512 devices in a mesh: dp: 4 (over x), expert: 64 (over z, y), half: 2 (over core).
Axes of the slice: x: 4, y: 4, z: 16, core: 2. Of those that a mesh axis runs over, the one named last changes fastest.
Arguments:
- activations: bfloat16 [2, 4096, 2048], P(None, ('dp', 'expert', 'half')), parts along dimension 1, may hold values from -6 to 6
- upstream: bfloat16 [2, 4096, 2048], P(None, ('dp', 'expert', 'half')), parts along dimension 1, may hold values from -12 to 12
- routes: int32 [2, 4096, 10], P(None, ('dp', 'expert', 'half')), parts along dimension 1, may hold values from 0 to 63, all different within a row; in each aligned block of 8 rows (0 to 7, 8 to 15, ..., all dimensions but the last counted through in order) at most 2 rows name the same one
- route_gates: float32 [2, 4096, 10], P(None, ('dp', 'expert', 'half')), parts along dimension 1, may hold values from 0.05 to 0.2
- gate_matrix: bfloat16 [64, 2048, 512], P('expert', None, 'half'), may hold values from -0.125 to 0.125
- up_matrix: bfloat16 [64, 2048, 512], P('expert', None, 'half'), may hold values from -3 to 3
- down_matrix: bfloat16 [64, 512, 2048], P('expert', 'half'), may hold values from -0.25 to 0.25
Outputs:
- input_cotangent: bfloat16 [2, 4096, 2048], P(None, ('dp', 'expert', 'half')), parts along dimension 1
- down_update: bfloat16 [256, 512, 2048], P(('dp', 'expert'), 'half'), parts along dimension 0
The draws below stay inside these ranges and needn't reach their ends.
There are 4 independent parts, one for each index of `dp`. The reference program is written for one: setup_inputs(seed, part) draws one part's arguments, and reference() takes and returns one part's arrays. A program takes and returns all parts, laid end to end along the dimension named above; an argument that names none is the same for every part. Nothing has to cross between parts.
Inputs may be any that keep to these rules, and one draw needn't show every extreme that they name: `routes`: each row names 10 different experts; within the rows of one device in one microbatch (aligned blocks of 8 rows) no expert is named more than 2 times, and in some blocks one expert is named exactly 2 times.
All inputs are finite; a program needn't handle non-finite values.
Results may differ from the reference program's by a relative error of at most 0.007.
Values may be sent and summed in bfloat16 or wider, within the bound.
A program may use at most 64 MiB of HBM per device.

```python
import math
import jax
import jax.numpy as jnp
import numpy as np
from jax import lax

D = 2048
FF = 512
MB = 2
ITERS = 2
TOK_MB = 8
EXPERTS = 64
TOP = 10
CAP = 2
TOKENS = 1024
N_HALF = 2


def draw_upstream(key, part):
    key_own, key_scale = jax.random.split(key, 2)
    column_scale = jnp.exp(jax.random.uniform(key_scale, (D,), jnp.float32) * jnp.log(10.0))
    values = 0.3 * jnp.clip(jax.random.normal(key_own, (MB, TOKENS, D), jnp.float32), -4.0, 4.0)
    return jnp.clip(values * column_scale[None, None, :], -12.0, 12.0).astype(jnp.bfloat16)


def draw_up_matrix(key, part):
    key_entry, key_jitter = jax.random.split(key)
    jitter = jax.random.uniform(key_jitter, (EXPERTS, 1, FF), jnp.float32)
    ladder = (jnp.arange(FF, dtype=jnp.float32)[None, None, :] + jitter) / FF
    column_scale = jnp.exp(ladder * jnp.log(10.0))
    entries = jnp.clip(jax.random.normal(key_entry, (EXPERTS, D, FF), jnp.float32), -4.0, 4.0)
    return jnp.clip(entries * column_scale / jnp.sqrt(1.0 * D), -3.0, 3.0).astype(jnp.bfloat16)


def steps_of(key, extent, pieces, low, high):
    level = 1.0
    for axis_at, blocks in pieces:
        draws = jax.random.uniform(jax.random.fold_in(jax.random.fold_in(key, 6), axis_at), (blocks,), jnp.float32, low / len(pieces), high / len(pieces))
        level = level * jnp.repeat(jnp.exp(draws), extent[axis_at] // blocks).reshape((-1,) + (1,) * (len(extent) - 1 - axis_at))
    return level


def shared_out(stream_key, own, number, rows, number_of, top, limit, lean):
    sequence = jax.random.permutation(stream_key, number_of)
    crowded, usual = portions_of(number_of, rows * top, limit, lean, True), portions_of(number_of, rows * top, limit, lean, False)
    places = jnp.arange(number_of)

    def named(sizes, rotation):
        used = int((sizes > 0).sum())
        fixed = max(1, used // 4)
        moved = fixed + (places - fixed + rotation * (used - fixed)) % max(1, number_of - fixed)
        return jnp.zeros((number_of,), jnp.int32).at[sequence[jnp.where(places < fixed, places, moved)]].set(jnp.asarray(sizes, jnp.int32))

    sizes = jnp.where(number % 4 == 0, named(crowded, number // 4), named(usual, number - number // 4 - 1))
    mixed = jax.random.permutation(jax.random.fold_in(own, 3), number_of)
    donor, taker = mixed[0:number_of // 2 * 2:2], mixed[1:number_of // 2 * 2:2]
    margin = jnp.minimum(sizes[donor] - 1, limit - sizes[taker]) // 2
    margin = jnp.where((donor == sequence[0]) | (taker == sequence[0]) | (sizes[taker] == 0), 0, jnp.maximum(margin, 0))
    moved = jax.random.randint(jax.random.fold_in(own, 4), (number_of // 2,), 0, 1 << 20) % (margin + 1)
    sizes = sizes.at[donor].add(-moved).at[taker].add(moved)
    members = jnp.searchsorted(jnp.cumsum(sizes), jnp.arange(rows * top), side="right").astype(jnp.int32)
    grid = members.reshape(top, rows).T
    grid = grid[jax.random.permutation(jax.random.fold_in(own, 1), rows)]
    rotation = jax.random.randint(jax.random.fold_in(own, 2), (rows, 1), 0, top)
    return jnp.take_along_axis(grid, (jnp.arange(top)[None, :] + rotation) % top, axis=1)


def portions_of(count, total, most, skew, full):
    loads = [(1 << 20) // math.isqrt(standing ** skew) + 1 for standing in range(1, count + 1)]
    largest = most if full else min(most, max(-(-total // count), total * loads[0] // sum(loads)))
    least = 1 if total - largest >= count - 1 else 0
    given, spare = [largest] + [least] * (count - 1), total - largest - least * (count - 1)
    while spare > 0:
        movable = [i for i in range(1, count) if given[i] < largest] or [i for i in range(1, count) if given[i] < most]
        whole, budget = sum([loads[i] for i in movable]), spare
        for i in movable:
            addition = min(most - given[i], max(1, budget * loads[i] // whole), spare)
            given[i] = given[i] + addition
            spare = spare - addition
    return np.array(given)


def centred(key, shape, spread, most, shards=(), kind=jnp.bfloat16):
    drawn = spread * jax.random.normal(key, shape, jnp.float32)
    if shards:
        drawn = drawn * steps_of(key, shape, shards, -0.22, 0.18)
    return jnp.clip(drawn, -most, most).astype(kind)


def setup_inputs(seed: int = 0, part: int = 0) -> dict:
    key_of = jax.random.split(jax.random.key(seed), 8)
    own_keys = jax.random.split(jax.random.fold_in(key_of[7], part), 8)
    activations = centred(own_keys[0], (MB, TOKENS, D), 1.0, 6.0, ((1, 128),))
    upstream = draw_upstream(jax.random.fold_in(jax.random.fold_in(key_of[7], part), 71), part)
    routes_keys = jax.random.split(jax.random.fold_in(own_keys[2], 1), MB * TOKENS // TOK_MB)
    routes_turns = jax.random.permutation(jax.random.fold_in(own_keys[2], 3), MB * TOKENS // TOK_MB)
    routes = jax.vmap(lambda own, number: shared_out(jax.random.fold_in(own_keys[2], 2), own, number, TOK_MB, EXPERTS, TOP, CAP, 2))(routes_keys, routes_turns).reshape((MB, TOKENS, TOP))
    route_gates = jnp.clip(0.05 + 0.15 * jax.random.uniform(own_keys[3], (MB, TOKENS, TOP), jnp.float32) ** steps_of(own_keys[3], (MB, TOKENS, TOP), ((1, 128),), -0.2, 0.2), 0.05, 0.2)
    gate_matrix = centred(key_of[4], (EXPERTS, D, FF), D ** -0.5, 0.125, ((0, 64), (2, 2)))
    up_matrix = draw_up_matrix(jax.random.fold_in(key_of[7], 71), part)
    down_matrix = centred(key_of[6], (EXPERTS, FF, D), FF ** -0.5, 0.25, ((0, 64), (1, 2)))
    return {"activations": activations, "upstream": upstream, "routes": routes, "route_gates": route_gates, "gate_matrix": gate_matrix, "up_matrix": up_matrix, "down_matrix": down_matrix}


linear_term = 3.4445
cubic_term = -4.775
quintic_term = 2.0315

def contract_last(left, right):
    return lax.dot_general(left, right, (((1,), (1,)), ((), ())), preferred_element_type=jnp.float32)

def contract_first(left, right):
    return lax.dot_general(left, right, (((0,), (0,)), ((), ())), preferred_element_type=jnp.float32)

def orthogonalize(down_grad):
    norm_value = jnp.sqrt(jnp.sum(down_grad * down_grad))
    current = down_grad / (norm_value + 1e-07)
    for iteration in range(ITERS):
        rounded = current.astype(jnp.bfloat16)
        gram_full = contract_last(rounded, rounded)
        gram_round = gram_full.astype(jnp.bfloat16)
        square_full = jnp.dot(gram_round, gram_round, preferred_element_type=jnp.float32)
        polynomial = (cubic_term * gram_full + quintic_term * square_full).astype(jnp.bfloat16)
        current = linear_term * current + jnp.dot(polynomial, rounded, preferred_element_type=jnp.float32)
    return (current * math.sqrt(max(FF, D))).astype(jnp.bfloat16)

def expert_step(inputs):
    token_rows, scaled_rows, gate_local, up_local, down_local = inputs
    pre_gate = jnp.dot(token_rows, gate_local, preferred_element_type=jnp.float32)
    pre_up = jnp.dot(token_rows, up_local, preferred_element_type=jnp.float32)
    sigmoid_gate = jax.nn.sigmoid(pre_gate)
    activated = pre_gate * sigmoid_gate
    hidden = (activated * pre_up).astype(jnp.bfloat16)
    hidden_grad = contract_last(scaled_rows, down_local)
    gate_grad = (hidden_grad * pre_up * sigmoid_gate * (1.0 + pre_gate * (1.0 - sigmoid_gate))).astype(jnp.bfloat16)
    up_grad = (hidden_grad * activated).astype(jnp.bfloat16)
    half_width = FF // N_HALF
    summed = jnp.zeros(token_rows.shape, jnp.float32)
    for half_index in range(N_HALF):
        lower = half_index * half_width
        upper = lower + half_width
        piece = contract_last(gate_grad[:, lower:upper], gate_local[:, lower:upper])
        piece = piece + contract_last(up_grad[:, lower:upper], up_local[:, lower:upper])
        summed = summed + lax.optimization_barrier(piece.astype(jnp.bfloat16)).astype(jnp.float32)
    entry_grad = summed.astype(jnp.bfloat16)
    down_grad = contract_first(hidden, scaled_rows)
    return (entry_grad, orthogonalize(down_grad))

def reference(activations, upstream, routes, route_gates, gate_matrix, up_matrix, down_matrix):
    blocks = MB * (TOKENS // TOK_MB)
    row_count = TOK_MB * TOP
    route_rows = routes.reshape(blocks, row_count)
    onehot = (route_rows[:, :, None] == jnp.arange(EXPERTS, dtype=jnp.int32)[None, None, :]).astype(jnp.int32)
    before = jnp.cumsum(onehot, axis=1) - onehot
    position = lax.optimization_barrier(jnp.sum(before * onehot, axis=2)).astype(jnp.int32)
    block_ids = jnp.arange(blocks, dtype=jnp.int32)[:, None]
    target = ((route_rows * blocks + block_ids) * CAP + position).reshape(blocks * row_count).astype(jnp.int32)
    token_ids = (block_ids * TOK_MB + jnp.arange(row_count, dtype=jnp.int32)[None, :] // TOP).reshape(blocks * row_count).astype(jnp.int32)
    flat_tokens = activations.reshape(MB * TOKENS, D)
    scaled = (route_gates[:, :, :, None] * upstream[:, :, None, :].astype(jnp.float32)).astype(jnp.bfloat16)
    scaled = scaled.reshape(MB * TOKENS * TOP, D)
    total = EXPERTS * blocks * CAP
    token_buffer = jnp.zeros((total, D), jnp.bfloat16).at[target].set(flat_tokens[token_ids])
    scaled_buffer = jnp.zeros((total, D), jnp.bfloat16).at[target].set(scaled)
    token_buffer = token_buffer.reshape(EXPERTS, blocks * CAP, D)
    scaled_buffer = scaled_buffer.reshape(EXPERTS, blocks * CAP, D)
    entry_rows, updates = lax.map(expert_step, (token_buffer, scaled_buffer, gate_matrix, up_matrix, down_matrix))
    per_entry = entry_rows.reshape(total, D)[target].astype(jnp.float32).reshape(MB * TOKENS, TOP, D)
    cotangent = lax.optimization_barrier(jnp.sum(per_entry, axis=1)).astype(jnp.bfloat16).reshape(MB, TOKENS, D)
    return (cotangent, updates)
```

```python
import functools
import math

import jax
import jax.numpy as jnp
from jax import lax
from jax.experimental import pallas as pl
from jax.experimental.pallas import tpu as pltpu
from jax.sharding import PartitionSpec as P

MESH = pl.DeviceIdType.MESH
NY = 4
ITERS = 2
LINEAR, CUBIC, QUINTIC = 3.4445, -4.775, 2.0315
F32, BF16 = jnp.float32, jnp.bfloat16


def nt(a, b, **kw):
    return lax.dot_general(
        a, b, (((1,), (1,)), ((), ())), preferred_element_type=F32, **kw
    )


def iota(shape, axis):
    return lax.broadcasted_iota(jnp.int32, shape, axis)


def run_both(first, second):
    live = [first, second]
    while live:
        for gen in list(live):
            try:
                next(gen)
            except StopIteration:
                live.remove(gen)


def kernel(
    NZ, act_ref, ups_ref, routes_ref, gates_ref, gate_hbm, up_hbm, down_hbm,
    cot_ref, cur_ref,
    zbuf, gbuf, ysend, ybuf, rows_tok, rows_sc, gu, down,
    part_own, part_send, part_recv, esend, ebuf, cbuf, rsend, rrecv,
    nsend, nrecv, whole, gram_b,
    w_sem, z_ss, z_rs, g_ss, g_rs, y_ss, y_rs, f_ss, f_rs, p_ss, p_rs, e_ss, e_rs,
    r_ss, r_rs, n_ss, n_rs, x_ss, x_rs, m_ss, m_rs,
):
    K = NZ // 2
    Q = K // 2
    D = zbuf.shape[-1]
    H = down.shape[0]
    D2 = D // 2
    TN = min(512, D)
    QG = rows_tok.shape[2]
    NG = Q // QG
    ex = lax.axis_index("expert")
    me = lax.axis_index("half")
    z = ex // NY
    y = ex % NY
    z_up = {"expert": ((z + 1) % NZ) * NY + y}
    z_dn = {"expert": ((z + NZ - 1) % NZ) * NY + y}
    z_to = (z_up, z_dn)
    y_to = [None] + [{"expert": z * NY + (y + r) % NY} for r in range(1, NY)]
    partner = {"half": 1 - me}
    pending = []

    def send(src, dst, ss, rs, dev):
        c = pltpu.make_async_remote_copy(
            src_ref=src, dst_ref=dst, send_sem=ss, recv_sem=rs,
            device_id=dev, device_id_type=MESH,
        )
        c.start()
        pending.append(c)

    def arrived(dst, rs, dev):
        pltpu.make_async_remote_copy(
            src_ref=dst, dst_ref=dst, send_sem=rs, recv_sem=rs,
            device_id=dev, device_id_type=MESH,
        ).wait_recv()

    weights = [
        pltpu.make_async_copy(gate_hbm.at[0], gu.at[:, pl.ds(0, H)], w_sem.at[0]),
        pltpu.make_async_copy(up_hbm.at[0], gu.at[:, pl.ds(H, H)], w_sem.at[1]),
        pltpu.make_async_copy(down_hbm.at[0], down, w_sem.at[2]),
    ]
    for w in weights:
        w.start()

    barrier = pltpu.get_barrier_semaphore()
    peers = [z_up, z_dn, partner] + y_to[1:]
    for p in peers:
        pl.semaphore_signal(barrier, inc=1, device_id=p, device_id_type=MESH)

    lane = iota((8, 128), 1)
    sub = iota((8, 128), 0)
    for m in range(2):
        zbuf[K - 1, 0, pl.ds(m * 16, 16), :] = jnp.concatenate(
            [act_ref[m].astype(F32), ups_ref[m].astype(F32)], axis=0
        ).astype(BF16)
        route = routes_ref[m]
        gate = gates_ref[m]
        gsum = jnp.zeros((8, 128), F32)
        named = jnp.zeros((8, 128), F32)
        for k in range(route.shape[1]):
            hit = route[:, k : k + 1] == lane // 2
            gsum = gsum + jnp.where(hit, gate[:, k : k + 1], 0.0)
            named = named + jnp.where(hit, 1.0, 0.0)
        before = jnp.zeros((8, 128), F32)
        for t in range(7):
            before = before + jnp.where(sub > t, named[t : t + 1, :], 0.0)
        gbuf[K - 1, 0, pl.ds(m * 8, 8), :] = jnp.where(
            before == (lane % 2).astype(F32), gsum, 0.0
        )

    pl.semaphore_wait(barrier, len(peers))

    def hop(s, d, key):
        buf = gbuf if key == "g" else zbuf
        src = buf.at[K - 1, 0] if s == 1 else buf.at[s - 2, d]
        dst = buf.at[s - 1, d] if s < K else buf.at[K - 1, 1]
        if key == "g":
            return src, dst, g_ss.at[d, s - 1], g_rs.at[d, s - 1], z_to[d]
        rows = pl.ds(key * 16, 16)
        ss, rs = z_ss.at[d, s - 1, key], z_rs.at[d, s - 1, key]
        return src.at[rows], dst.at[rows], ss, rs, z_to[d]

    def goes(s, d, key):
        return s < K or (s == K and (d == 0 if key == "g" else key == d))

    pieces = [(d, key) for key in ("g", 0, 1) for d in range(2)]
    for d, key in pieces:
        send(*hop(1, d, key))

    r64, c64 = iota((64, 64), 0), iota((64, 64), 1)
    e_row, e_lane = iota((64, 128), 0), iota((64, 128), 1)
    slot_of_row = 2 * (z * NY + (y + e_row // 16) % NY) + e_row % 2
    pick = jnp.where(e_lane == slot_of_row, 1.0, 0.0)
    block_of_row = ((r64 // 4) % 2) * 4 + ((r64 // 2) % 2) * 2 + (r64 // 8) % 2
    same_block = c64 // 8 == block_of_row
    scaled_row = (iota((64, 1), 0) // 8) % 2 == 1

    def select(i):
        ga, gb = gbuf[i, 0], gbuf[i, 1]
        tokens = jnp.concatenate(
            [ga[:8], ga[:8], ga[8:], ga[8:], gb[:8], gb[:8], gb[8:], gb[8:]], axis=0
        )
        table = nt(pick, tokens, precision=lax.Precision.HIGHEST)
        table = jnp.where(same_block, table, 0.0)
        scale = jnp.where(scaled_row, jnp.sum(table, axis=1, keepdims=True), 1.0)
        chosen = jnp.where(table > 0.0, 1.0, 0.0).astype(BF16)
        for n in range(0, D, TN):
            x = zbuf[i, :, :, pl.ds(n, TN)].reshape(64, TN)
            picked = jnp.dot(chosen, x, preferred_element_type=F32) * scale
            picked = picked.astype(BF16)
            ybuf[0, i, 0, :, pl.ds(n, TN)] = picked[:16]
            ysend[i, :, :, pl.ds(n, TN)] = picked[16:].reshape(NY - 1, 16, TN)
        for r in range(1, NY):
            send(
                ysend.at[i, r - 1], ybuf.at[0, i, NY - r],
                y_ss.at[i, r - 1], y_rs.at[i, r - 1], y_to[r],
            )

    def pass_on(i):
        for r in range(1, NY):
            arrived(ybuf.at[0, i, NY - r], y_rs.at[i, r - 1], y_to[r])
        send(ybuf.at[0, i], ybuf.at[1, i], f_ss.at[i], f_rs.at[i], partner)

    def part_rows(q, lane_of):
        g, qq = q // QG, q % QG
        for r in range(NY):
            for n in range(0, D, TN):
                two = ybuf[lane_of, pl.ds(2 * q, 2), r, :, pl.ds(n, TN)].astype(F32)
                at = pl.ds(r * 16, 16)
                rows_tok[g, lane_of, qq, at, pl.ds(n, TN)] = jnp.concatenate(
                    [two[0, :8], two[1, :8]], axis=0
                ).astype(BF16)
                rows_sc[g, lane_of, qq, at, pl.ds(n, TN)] = jnp.concatenate(
                    [two[0, 8:], two[1, 8:]], axis=0
                ).astype(BF16)

    def expert(g):
        rows = 2 * QG * 64
        tok = rows_tok[g].reshape(rows, D)
        sc = rows_sc[g].reshape(rows, D)
        pre = jnp.dot(tok, gu[...], preferred_element_type=F32)
        pre_gate, pre_up = pre[:, :H], pre[:, H:]
        sig = jax.nn.sigmoid(pre_gate)
        activated = pre_gate * sig
        hidden = activated * pre_up
        hidden_grad = nt(sc, down[...])
        gate_grad = hidden_grad * pre_up * sig * (1.0 + pre_gate * (1.0 - sig))
        both = jnp.concatenate(
            [gate_grad.astype(BF16), (hidden_grad * activated).astype(BF16)], axis=1
        )
        for n in range(0, D, TN):
            part = nt(both, gu[pl.ds(n, TN), :]).astype(BF16)
            part = part.reshape(2, QG, 64, TN)
            part_own[g, :, :, pl.ds(n, TN)] = part[0]
            part_send[g, :, :, pl.ds(n, TN)] = part[1]
        for qq in range(QG):
            send(
                part_send.at[g, qq], part_recv.at[g, qq],
                p_ss.at[g, qq], p_rs.at[g, qq], partner,
            )
        turned = hidden.T.astype(BF16)
        for n in range(0, D, TN):
            at = pl.ds(n, TN)
            sc_n = rows_sc[g, :, :, :, at].reshape(rows, TN)
            grad = jnp.dot(turned, sc_n, preferred_element_type=F32)
            cur_ref[:, at] = grad if g == 0 else cur_ref[:, at] + grad

    def give_back(q):
        g, qq = q // QG, q % QG
        arrived(part_recv.at[g, qq], p_rs.at[g, qq], partner)
        for n in range(0, D, TN):
            at = pl.ds(n, TN)
            total = part_own[g, qq, :, at].astype(F32) + part_recv[g, qq, :, at].astype(F32)
            total = total.astype(BF16)
            ebuf[q, 0, :, at] = total[:16]
            esend[q, :, :, at] = total[16:].reshape(NY - 1, 16, TN)
        for r in range(1, NY):
            send(
                esend.at[q, r - 1], ebuf.at[q, NY - r],
                e_ss.at[q, r - 1], e_rs.at[q, r - 1], y_to[r],
            )

    def combine(q):
        for r in range(1, NY):
            arrived(ebuf.at[q, NY - r], e_rs.at[q, r - 1], y_to[r])
        tokens = gbuf[pl.ds(2 * q, 2)].reshape(64, 128)
        table = nt(tokens, pick, precision=lax.Precision.HIGHEST)
        mine = (r64 // 8 == (c64 // 2) % 8) & (table > 0.0)
        chosen = jnp.where(mine, 1.0, 0.0).astype(BF16)
        for n in range(0, D, TN):
            x = ebuf[q, :, :, pl.ds(n, TN)].reshape(64, TN)
            total = jnp.dot(chosen, x, preferred_element_type=F32)
            cbuf[pl.ds(2 * q, 2), :, :, pl.ds(n, TN)] = total.reshape(2, 2, 16, TN)

    def ring(s, d, c):
        at = pl.ds(c * D2, D2)
        ss, rs = r_ss.at[d, s - 1, c], r_rs.at[d, s - 1, c]
        return rsend.at[d, s - 1, :, at], rrecv.at[d, s - 1, :, at], ss, rs, z_to[d]

    def sum_z():
        for c in range(2):
            rsend[c, 0, :, pl.ds(c * D2, D2)] = cbuf[K - 1, 1, :, pl.ds(c * D2, D2)].astype(BF16)
            send(*ring(1, c, c))
        yield
        for s in range(2, K + 1):
            for c in range(2):
                for d in range(2):
                    at = pl.ds(c * D2, D2)
                    total = cbuf[K - s, 1 - d, :, at]
                    if s > 2 or c == d:
                        _, dst, _, rs, dev = ring(s - 1, d, c)
                        arrived(dst, rs, dev)
                        total = total + rrecv[d, s - 2, :, at].astype(F32)
                    rsend[d, s - 1, :, at] = total.astype(BF16)
                    send(*ring(s, d, c))
            yield
        for c in range(2):
            at = pl.ds(c * D2, D2)
            total = cbuf[K - 1, 0, :, at]
            for d in range(2):
                _, dst, _, rs, dev = ring(K, d, c)
                arrived(dst, rs, dev)
                total = total + rrecv[d, K - 1, :, at].astype(F32)
            cot_ref[:, at] = total
        yield

    def newton():
        squares = jnp.zeros((8, 128), F32)
        for n in range(0, D, 128):
            piece = cur_ref[:, pl.ds(n, 128)]
            squares = squares + jnp.sum((piece * piece).reshape(H // 8, 8, 128), axis=0)
        nsend[...] = jnp.broadcast_to(jnp.sum(squares, keepdims=True), (8, 128))
        send(nsend, nrecv, n_ss, n_rs, partner)
        arrived(nrecv, n_rs, partner)
        yield
        norm = jnp.sqrt(nsend[...] + nrecv[...]) + 1e-07
        factor = (1.0 / norm)[:1, :1]
        for it in range(ITERS):
            mine = whole.at[it, me]
            for n in range(0, D, TN):
                at = pl.ds(n, TN)
                if it == 0:
                    value = cur_ref[:, at] * factor
                    cur_ref[:, at] = value
                    mine[:, at] = value.astype(BF16)
            send(mine, mine, x_ss.at[it], x_rs.at[it], partner)
            yield
            other = whole.at[it, 1 - me]
            gram_own = nt(mine[...], mine[...])
            yield
            arrived(other, x_rs.at[it], partner)
            gram_other = nt(mine[...], other[...])
            gm = gram_b.at[it, me]
            own_at = pl.ds(pl.multiple_of(me * H, H), H)
            other_at = pl.ds(pl.multiple_of((1 - me) * H, H), H)
            gm[:, own_at] = gram_own.astype(BF16)
            gm[:, other_at] = gram_other.astype(BF16)
            send(gm, gm, m_ss.at[it], m_rs.at[it], partner)
            yield
            arrived(gram_b.at[it, 1 - me], m_rs.at[it], partner)
            full = gram_b[it].reshape(2 * H, 2 * H)
            square = jnp.dot(gm[...], full, preferred_element_type=F32)
            sq_own = jnp.where(me == 0, square[:, :H], square[:, H:])
            sq_other = jnp.where(me == 0, square[:, H:], square[:, :H])
            p_own = (CUBIC * gram_own + QUINTIC * sq_own).astype(BF16)
            p_other = (CUBIC * gram_other + QUINTIC * sq_other).astype(BF16)
            yield
            for n in range(0, D, TN):
                at = pl.ds(n, TN)
                step = jnp.dot(p_own, mine[:, at], preferred_element_type=F32)
                step = step + jnp.dot(p_other, other[:, at], preferred_element_type=F32)
                value = LINEAR * cur_ref[:, at] + step
                cur_ref[:, at] = value
                if it + 1 < ITERS:
                    whole.at[it + 1, me][:, at] = value.astype(BF16)
            yield

    for s in range(1, K + 1):
        for d, key in pieces:
            if goes(s, d, key):
                arrived(*hop(s, d, key)[1::2], z_to[d])
                if goes(s + 1, d, key):
                    send(*hop(s + 1, d, key))
        select(s - 1)
        if s > 1:
            pass_on(s - 2)
        if s > 2:
            arrived(ybuf.at[1, s - 3], f_rs.at[s - 3], partner)
            if s % 2 == 0:
                for lane_of in range(2):
                    part_rows(s // 2 - 2, lane_of)
        if s == 1:
            for w in weights:
                w.wait()
    arrived(ybuf.at[1, K - 2], f_rs.at[K - 2], partner)
    pass_on(K - 1)
    for g in range(NG - 1):
        expert(g)
        for qq in range(QG):
            give_back(g * QG + qq)
    arrived(ybuf.at[1, K - 1], f_rs.at[K - 1], partner)
    for lane_of in range(2):
        part_rows(Q - 1, lane_of)
    expert(NG - 1)
    for qq in reversed(range(QG)):
        give_back((NG - 1) * QG + qq)
    for q in reversed(range(Q)):
        combine(q)
    run_both(sum_z(), newton())
    for c in pending:
        c.wait_send()


def on_device(activations, upstream, routes, route_gates, gate_matrix, up_matrix, down_matrix):
    NZ = lax.axis_size("expert") // NY
    K = NZ // 2
    Q = K // 2
    D = activations.shape[2]
    H = down_matrix.shape[1]
    QG = max(1, Q // 2)
    NG = Q // QG
    dma = pltpu.SemaphoreType.DMA
    vmem = pl.BlockSpec(memory_space=pltpu.VMEM)
    anywhere = pl.BlockSpec(memory_space=pl.ANY)
    cot, cur = pl.pallas_call(
        functools.partial(kernel, NZ),
        out_shape=(
            jax.ShapeDtypeStruct((16, D), F32),
            jax.ShapeDtypeStruct((H, D), F32),
        ),
        in_specs=[vmem] * 4 + [anywhere] * 3,
        out_specs=(vmem, vmem),
        scratch_shapes=[
            pltpu.VMEM((K, 2, 32, D), BF16),
            pltpu.VMEM((K, 2, 16, 128), F32),
            pltpu.VMEM((K, NY - 1, 16, D), BF16),
            pltpu.VMEM((2, K, NY, 16, D), BF16),
            pltpu.VMEM((NG, 2, QG, 64, D), BF16),
            pltpu.VMEM((NG, 2, QG, 64, D), BF16),
            pltpu.VMEM((D, 2 * H), BF16),
            pltpu.VMEM((H, D), BF16),
            pltpu.VMEM((NG, QG, 64, D), BF16),
            pltpu.VMEM((NG, QG, 64, D), BF16),
            pltpu.VMEM((NG, QG, 64, D), BF16),
            pltpu.VMEM((Q, NY - 1, 16, D), BF16),
            pltpu.VMEM((Q, NY, 16, D), BF16),
            pltpu.VMEM((K, 2, 16, D), F32),
            pltpu.VMEM((2, K, 16, D), BF16),
            pltpu.VMEM((2, K, 16, D), BF16),
            pltpu.VMEM((8, 128), F32),
            pltpu.VMEM((8, 128), F32),
            pltpu.VMEM((ITERS, 2, H, D), BF16),
            pltpu.VMEM((ITERS, 2, H, 2 * H), BF16),
            dma((3,)),
            dma((2, K, 2)), dma((2, K, 2)),
            dma((2, K)), dma((2, K)),
            dma((K, NY - 1)), dma((K, NY - 1)),
            dma((K,)), dma((K,)),
            dma((NG, QG)), dma((NG, QG)),
            dma((Q, NY - 1)), dma((Q, NY - 1)),
            dma((2, K, 2)), dma((2, K, 2)),
            dma(()), dma(()),
            dma((ITERS,)), dma((ITERS,)),
            dma((ITERS,)), dma((ITERS,)),
        ],
        compiler_params=pltpu.CompilerParams(collective_id=0, has_side_effects=True),
    )(activations, upstream, routes, route_gates, gate_matrix, up_matrix, down_matrix)
    update = (cur * math.sqrt(max(2 * H, D))).astype(BF16)
    return (cot.astype(BF16).reshape(2, 8, D), update[None])


def solution(mesh):
    rows = P(None, ("dp", "expert", "half"), None)
    return jax.shard_map(
        on_device,
        mesh=mesh,
        in_specs=(
            rows, rows, rows, rows,
            P("expert", None, "half"), P("expert", None, "half"), P("expert", "half", None),
        ),
        out_specs=(rows, P(("dp", "expert"), "half", None)),
        check_vma=False,
    )
```

```python
import functools
import math

import jax
import jax.numpy as jnp
from jax import lax
from jax.experimental import pallas as pl
from jax.experimental.pallas import tpu as pltpu
from jax.sharding import PartitionSpec as P

MESH = pl.DeviceIdType.MESH
NY = 4
ITERS = 2
LINEAR, CUBIC, QUINTIC = 3.4445, -4.775, 2.0315
F32, BF16 = jnp.float32, jnp.bfloat16


def nt(a, b, **kw):
    return lax.dot_general(
        a, b, (((1,), (1,)), ((), ())), preferred_element_type=F32, **kw
    )


def iota(shape, axis):
    return lax.broadcasted_iota(jnp.int32, shape, axis)


def advance(gen, steps):
    for _ in range(steps):
        next(gen, None)


def kernel(
    NZ, act_hbm, ups_hbm, routes_hbm, gates_hbm, gate_hbm, up_hbm, down_hbm,
    cot_hbm, upd_hbm,
    act_ref, ups_ref, routes_ref, gates_ref, cot_ref, upd_ref, cur_ref, hid_t,
    zbuf, gbuf, ysend, ybuf, rows_tok, rows_sc, gu, down,
    part_own, part_send, part_recv, esend, ebuf, cbuf, rsend, rrecv,
    nsend, nrecv, whole, gram_b,
    w_sem, o_sem, z_ss, z_rs, g_ss, g_rs, y_ss, y_rs, f_ss, f_rs, p_ss, p_rs, e_ss, e_rs,
    r_ss, r_rs, n_ss, n_rs, x_ss, x_rs, m_ss, m_rs,
):
    K = NZ // 2
    Q = K // 2
    D = zbuf.shape[-1]
    H = down.shape[0]
    D2 = D // 2
    TN = min(512, D)
    ex = lax.axis_index("expert")
    me = lax.axis_index("half")
    z = ex // NY
    y = ex % NY
    z_up = {"expert": ((z + 1) % NZ) * NY + y}
    z_dn = {"expert": ((z + NZ - 1) % NZ) * NY + y}
    z_to = (z_up, z_dn)
    z_two = tuple({"expert": ((z + NZ + h) % NZ) * NY + y} for h in (2, -2))
    y_to = [None] + [{"expert": z * NY + (y + r) % NY} for r in range(1, NY)]
    partner = {"half": 1 - me}
    pending = []

    def send(src, dst, ss, rs, dev):
        c = pltpu.make_async_remote_copy(
            src_ref=src, dst_ref=dst, send_sem=ss, recv_sem=rs,
            device_id=dev, device_id_type=MESH,
        )
        c.start()
        pending.append(c)

    def arrived(dst, rs, dev):
        pltpu.make_async_remote_copy(
            src_ref=dst, dst_ref=dst, send_sem=rs, recv_sem=rs,
            device_id=dev, device_id_type=MESH,
        ).wait_recv()

    barrier = pltpu.get_barrier_semaphore()
    peers = [z_up, z_dn, *z_two, partner] + y_to[1:]
    for p in peers:
        pl.semaphore_signal(barrier, inc=1, device_id=p, device_id_type=MESH)

    loads = [
        pltpu.make_async_copy(src, dst, w_sem.at[n])
        for n, (src, dst) in enumerate(
            [
                (routes_hbm, routes_ref),
                (gates_hbm, gates_ref),
                (act_hbm, act_ref),
                (ups_hbm, ups_ref),
                (gate_hbm.at[0], gu.at[:, pl.ds(0, H)]),
                (up_hbm.at[0], gu.at[:, pl.ds(H, H)]),
                (down_hbm.at[0], down),
            ]
        )
    ]
    for c in loads:
        c.start()
    for c in loads[:4]:
        c.wait()

    lane = iota((8, 128), 1)
    sub = iota((8, 128), 0)
    for m in range(2):
        zbuf[K - 1, 0, pl.ds(m * 16, 16), :] = jnp.concatenate(
            [act_ref[m].astype(F32), ups_ref[m].astype(F32)], axis=0
        ).astype(BF16)
        route = routes_ref[m]
        gate = gates_ref[m]
        gsum = jnp.zeros((8, 128), F32)
        named = jnp.zeros((8, 128), F32)
        for k in range(route.shape[1]):
            hit = route[:, k : k + 1] == lane // 2
            gsum = gsum + jnp.where(hit, gate[:, k : k + 1], 0.0)
            named = named + jnp.where(hit, 1.0, 0.0)
        before = jnp.zeros((8, 128), F32)
        for t in range(7):
            before = before + jnp.where(sub > t, named[t : t + 1, :], 0.0)
        gbuf[K - 1, 0, pl.ds(m * 8, 8), :] = jnp.where(
            before == (lane % 2).astype(F32), gsum, 0.0
        )

    pl.semaphore_wait(barrier, len(peers))

    def hop(s, d, key):
        buf = gbuf if key == "g" else zbuf
        src = buf.at[K - 1, 0] if s == 1 else buf.at[s - 2, d]
        dst = buf.at[s - 1, d] if s < K else buf.at[K - 1, 1]
        if key == "g":
            return src, dst, g_ss.at[d, s - 1], g_rs.at[d, s - 1], z_to[d]
        m, c = key
        at = (pl.ds(m * 16, 16), pl.ds(c * D2, D2))
        ss, rs = z_ss.at[d, s - 1, 2 * m + c], z_rs.at[d, s - 1, 2 * m + c]
        return src.at[at], dst.at[at], ss, rs, z_to[d]

    def goes(s, d, key):
        return s < K or (s == K and (d == 0 if key == "g" else key[0] == d))

    halves = [(m, c) for m in range(2) for c in range(2)]
    pieces = [(d, key) for key in halves + ["g"] for d in range(2)]
    for d, key in pieces:
        send(*hop(1, d, key))

    r64, c64 = iota((64, 64), 0), iota((64, 64), 1)
    e_row, e_lane = iota((64, 128), 0), iota((64, 128), 1)
    slot_of_row = 2 * (z * NY + (y + e_row // 16) % NY) + e_row % 2
    pick = jnp.where(e_lane == slot_of_row, 1.0, 0.0)
    block_of_row = ((r64 // 4) % 2) * 4 + ((r64 // 2) % 2) * 2 + (r64 // 8) % 2
    same_block = c64 // 8 == block_of_row
    scaled_row = (iota((64, 1), 0) // 8) % 2 == 1

    def select(i):
        ga, gb = gbuf[i, 0], gbuf[i, 1]
        tokens = jnp.concatenate(
            [ga[:8], ga[:8], ga[8:], ga[8:], gb[:8], gb[:8], gb[8:], gb[8:]], axis=0
        )
        table = nt(pick, tokens, precision=lax.Precision.HIGHEST)
        table = jnp.where(same_block, table, 0.0)
        scale = jnp.where(scaled_row, jnp.sum(table, axis=1, keepdims=True), 1.0)
        chosen = jnp.where(table > 0.0, 1.0, 0.0).astype(BF16)
        for n in range(0, D, TN):
            x = zbuf[i, :, :, pl.ds(n, TN)].reshape(64, TN)
            picked = jnp.dot(chosen, x, preferred_element_type=F32) * scale
            picked = picked.astype(BF16)
            ybuf[0, i, 0, :, pl.ds(n, TN)] = picked[:16]
            ysend[i, :, :, pl.ds(n, TN)] = picked[16:].reshape(NY - 1, 16, TN)
        for r in range(1, NY):
            send(
                ysend.at[i, r - 1], ybuf.at[0, i, NY - r],
                y_ss.at[i, r - 1], y_rs.at[i, r - 1], y_to[r],
            )

    def pass_on(i):
        for r in range(1, NY):
            arrived(ybuf.at[0, i, NY - r], y_rs.at[i, r - 1], y_to[r])
        send(ybuf.at[0, i], ybuf.at[1, i], f_ss.at[i], f_rs.at[i], partner)

    def part_rows(q):
        for lane_of in range(2):
            for r in range(NY):
                for n in range(0, D, TN):
                    two = ybuf[lane_of, pl.ds(2 * q, 2), r, :, pl.ds(n, TN)].astype(F32)
                    at = pl.ds(r * 16, 16)
                    rows_tok[q, lane_of, at, pl.ds(n, TN)] = jnp.concatenate(
                        [two[0, :8], two[1, :8]], axis=0
                    ).astype(BF16)
                    rows_sc[q, lane_of, at, pl.ds(n, TN)] = jnp.concatenate(
                        [two[0, 8:], two[1, 8:]], axis=0
                    ).astype(BF16)

    def expert(q, nq):
        rows = nq * 128
        tok = rows_tok[pl.ds(q, nq)].reshape(rows, D)
        sc = rows_sc[pl.ds(q, nq)].reshape(rows, D)
        pre = jnp.dot(tok, gu[...], preferred_element_type=F32)
        pre_gate, pre_up = pre[:, :H], pre[:, H:]
        sig = jax.nn.sigmoid(pre_gate)
        activated = pre_gate * sig
        hidden = activated * pre_up
        hidden_grad = nt(sc, down[...])
        gate_grad = hidden_grad * pre_up * sig * (1.0 + pre_gate * (1.0 - sig))
        both = jnp.concatenate(
            [gate_grad.astype(BF16), (hidden_grad * activated).astype(BF16)], axis=1
        )
        for n in range(0, D, TN):
            part = nt(both, gu[pl.ds(n, TN), :]).astype(BF16)
            part = part.reshape(nq, 2, 64, TN)
            part_own[pl.ds(q, nq), :, pl.ds(n, TN)] = part[:, 0]
            part_send[pl.ds(q, nq), :, pl.ds(n, TN)] = part[:, 1]
        for p in range(q, q + nq):
            send(part_send.at[p], part_recv.at[p], p_ss.at[p], p_rs.at[p], partner)
        hid_t[:, pl.ds(q * 128, rows)] = hidden.T.astype(BF16)

    def down_grad():
        for n in range(0, D, TN):
            at = pl.ds(n, TN)
            sc_n = rows_sc[:, :, :, at].reshape(Q * 128, TN)
            cur_ref[:, at] = jnp.dot(hid_t[...], sc_n, preferred_element_type=F32)

    def give_back(q):
        arrived(part_recv.at[q], p_rs.at[q], partner)
        for n in range(0, D, TN):
            at = pl.ds(n, TN)
            total = part_own[q, :, at].astype(F32) + part_recv[q, :, at].astype(F32)
            total = total.astype(BF16)
            ebuf[q, 0, :, at] = total[:16]
            esend[q, :, :, at] = total[16:].reshape(NY - 1, 16, TN)
        for r in range(1, NY):
            send(
                esend.at[q, r - 1], ebuf.at[q, NY - r],
                e_ss.at[q, r - 1], e_rs.at[q, r - 1], y_to[r],
            )

    def combine(q):
        for r in range(1, NY):
            arrived(ebuf.at[q, NY - r], e_rs.at[q, r - 1], y_to[r])
        tokens = gbuf[pl.ds(2 * q, 2)].reshape(64, 128)
        table = nt(tokens, pick, precision=lax.Precision.HIGHEST)
        mine = (r64 // 8 == (c64 // 2) % 8) & (table > 0.0)
        chosen = jnp.where(mine, 1.0, 0.0).astype(BF16)
        for n in range(0, D, TN):
            x = ebuf[q, :, :, pl.ds(n, TN)].reshape(64, TN)
            total = jnp.dot(chosen, x, preferred_element_type=F32)
            cbuf[pl.ds(2 * q, 2), :, :, pl.ds(n, TN)] = total.reshape(2, 2, 16, TN)

    def chain(s, d, o, c):
        at = pl.ds(c * D2, D2)
        sem = (d, o, s - 1, c)
        dev = z_to[d] if o == 1 and s == Q else z_two[d]
        buf = (d, o, s - 1, slice(None), at)
        return rsend.at[buf], rrecv.at[buf], r_ss.at[sem], r_rs.at[sem], dev

    def joins(s, d, o, c):
        return s > 1 or o == 1 or c == d

    def sum_z():
        for s in range(1, Q + 1):
            for o in range(2):
                for c in range(2):
                    for d in range(2):
                        if not joins(s, d, o, c):
                            continue
                        at = pl.ds(c * D2, D2)
                        k = K + 2 - 2 * s - o
                        total = cbuf[k - 1, 1 if k == K else 1 - d, :, at]
                        if s > 1 and joins(s - 1, d, o, c):
                            _, dst, _, rs, dev = chain(s - 1, d, o, c)
                            arrived(dst, rs, dev)
                            total = total + rrecv[d, o, s - 2, :, at].astype(F32)
                        rsend[d, o, s - 1, :, at] = total.astype(BF16)
                        send(*chain(s, d, o, c))
            yield
        for c in range(2):
            at = pl.ds(c * D2, D2)
            total = cbuf[K - 1, 0, :, at]
            for o in range(2):
                for d in range(2):
                    if joins(Q, d, o, c):
                        _, dst, _, rs, dev = chain(Q, d, o, c)
                        arrived(dst, rs, dev)
                        total = total + rrecv[d, o, Q - 1, :, at].astype(F32)
            cot_ref[:, :, at] = total.reshape(2, 8, D2).astype(BF16)
        yield

    def newton():
        squares = jnp.zeros((8, 128), F32)
        for n in range(0, D, 128):
            piece = cur_ref[:, pl.ds(n, 128)]
            squares = squares + jnp.sum((piece * piece).reshape(H // 8, 8, 128), axis=0)
        nsend[...] = jnp.broadcast_to(jnp.sum(squares, keepdims=True), (8, 128))
        send(nsend, nrecv, n_ss, n_rs, partner)
        arrived(nrecv, n_rs, partner)
        yield
        norm = jnp.sqrt(nsend[...] + nrecv[...]) + 1e-07
        factor = (1.0 / norm)[:1, :1]
        for it in range(ITERS):
            mine = whole.at[it, me]
            for n in range(0, D, TN):
                at = pl.ds(n, TN)
                if it == 0:
                    value = cur_ref[:, at] * factor
                    cur_ref[:, at] = value
                    mine[:, at] = value.astype(BF16)
            send(mine, mine, x_ss.at[it], x_rs.at[it], partner)
            yield
            other = whole.at[it, 1 - me]
            gram_own = nt(mine[...], mine[...])
            yield
            arrived(other, x_rs.at[it], partner)
            gram_other = nt(mine[...], other[...])
            gm = gram_b.at[it, me]
            own_at = pl.ds(pl.multiple_of(me * H, H), H)
            other_at = pl.ds(pl.multiple_of((1 - me) * H, H), H)
            gm[:, own_at] = gram_own.astype(BF16)
            gm[:, other_at] = gram_other.astype(BF16)
            send(gm, gm, m_ss.at[it], m_rs.at[it], partner)
            yield
            arrived(gram_b.at[it, 1 - me], m_rs.at[it], partner)
            full = gram_b[it].reshape(2 * H, 2 * H)
            square = jnp.dot(gm[...], full, preferred_element_type=F32)
            sq_own = jnp.where(me == 0, square[:, :H], square[:, H:])
            sq_other = jnp.where(me == 0, square[:, H:], square[:, :H])
            p_own = (CUBIC * gram_own + QUINTIC * sq_own).astype(BF16)
            p_other = (CUBIC * gram_other + QUINTIC * sq_other).astype(BF16)
            yield
            for n in range(0, D, TN):
                at = pl.ds(n, TN)
                step = jnp.dot(p_own, mine[:, at], preferred_element_type=F32)
                step = step + jnp.dot(p_other, other[:, at], preferred_element_type=F32)
                value = LINEAR * cur_ref[:, at] + step
                if it + 1 < ITERS:
                    cur_ref[:, at] = value
                    whole.at[it + 1, me][:, at] = value.astype(BF16)
                else:
                    upd_ref[:, at] = (value * math.sqrt(max(2 * H, D))).astype(BF16)
            yield
        pltpu.make_async_copy(upd_ref, upd_hbm, o_sem.at[0]).start()

    def passed(i):
        arrived(ybuf.at[1, i], f_rs.at[i], partner)

    for s in range(1, K + 1):
        for d, key in pieces:
            if goes(s, d, key):
                arrived(*hop(s, d, key)[1::2], z_to[d])
                if goes(s + 1, d, key):
                    send(*hop(s + 1, d, key))
        select(s - 1)
        if s > 2:
            pass_on(s - 3)
        if s > 4 and s % 2 == 1:
            passed(s - 5)
            passed(s - 4)
            part_rows((s - 5) // 2)
    for w in loads[4:]:
        w.wait()
    for i in range(max(0, K - 2), K - 1):
        pass_on(i)
    if Q > 2:
        passed(K - 4)
        passed(K - 3)
        first = Q - 2
        for q in range(max(0, (K - 1 - 5) // 2 + 1), first + 1):
            if q < first:
                passed(2 * q)
                passed(2 * q + 1)
            part_rows(q)
        expert(0, first)
    pass_on(K - 1)
    if Q > 2:
        for q in range(first):
            give_back(q)
    if Q > 1:
        if Q == 2:
            passed(0)
            passed(1)
            part_rows(0)
        expert(Q - 2, 1)
    passed(K - 2)
    passed(K - 1)
    part_rows(Q - 1)
    expert(Q - 1, 1)
    down_grad()
    ns = newton()
    give_back(Q - 1)
    if Q > 1:
        give_back(Q - 2)
    for q in range(Q - 2):
        combine(q)
    advance(ns, 2)
    combine(Q - 1)
    ring = sum_z()
    advance(ring, 1)
    if Q > 1:
        combine(Q - 2)
    for s in range(2, Q + 1):
        advance(ns, 3)
        advance(ring, 1)
    advance(ns, 20)
    advance(ring, 2)
    cot_out = pltpu.make_async_copy(cot_ref, cot_hbm, o_sem.at[1])
    cot_out.start()
    for c in pending:
        c.wait_send()
    cot_out.wait()
    pltpu.make_async_copy(upd_ref, upd_hbm, o_sem.at[0]).wait()


def hand_over(cot_ref, upd_ref, cot_out, upd_out):
    cot_out[...] = cot_ref[...]
    upd_out[...] = upd_ref[...]


def on_device(activations, upstream, routes, route_gates, gate_matrix, up_matrix, down_matrix):
    NZ = lax.axis_size("expert") // NY
    K = NZ // 2
    Q = K // 2
    D = activations.shape[2]
    H = down_matrix.shape[1]
    dma = pltpu.SemaphoreType.DMA
    anywhere = pl.BlockSpec(memory_space=pl.ANY)
    args = (activations, upstream, routes, route_gates, gate_matrix, up_matrix, down_matrix)
    cot, upd = pl.pallas_call(
        functools.partial(kernel, NZ),
        out_shape=(
            jax.ShapeDtypeStruct((2, 8, D), BF16),
            jax.ShapeDtypeStruct((H, D), BF16),
        ),
        in_specs=[anywhere] * 7,
        out_specs=(anywhere, anywhere),
        scratch_shapes=[
            pltpu.VMEM(activations.shape, BF16),
            pltpu.VMEM(upstream.shape, BF16),
            pltpu.VMEM(routes.shape, routes.dtype),
            pltpu.VMEM(route_gates.shape, F32),
            pltpu.VMEM((2, 8, D), BF16),
            pltpu.VMEM((H, D), BF16),
            pltpu.VMEM((H, D), F32),
            pltpu.VMEM((H, Q * 128), BF16),
            pltpu.VMEM((K, 2, 32, D), BF16),
            pltpu.VMEM((K, 2, 16, 128), F32),
            pltpu.VMEM((K, NY - 1, 16, D), BF16),
            pltpu.VMEM((2, K, NY, 16, D), BF16),
            pltpu.VMEM((Q, 2, 64, D), BF16),
            pltpu.VMEM((Q, 2, 64, D), BF16),
            pltpu.VMEM((D, 2 * H), BF16),
            pltpu.VMEM((H, D), BF16),
            pltpu.VMEM((Q, 64, D), BF16),
            pltpu.VMEM((Q, 64, D), BF16),
            pltpu.VMEM((Q, 64, D), BF16),
            pltpu.VMEM((Q, NY - 1, 16, D), BF16),
            pltpu.VMEM((Q, NY, 16, D), BF16),
            pltpu.VMEM((K, 2, 16, D), F32),
            pltpu.VMEM((2, 2, Q, 16, D), BF16),
            pltpu.VMEM((2, 2, Q, 16, D), BF16),
            pltpu.VMEM((8, 128), F32),
            pltpu.VMEM((8, 128), F32),
            pltpu.VMEM((ITERS, 2, H, D), BF16),
            pltpu.VMEM((ITERS, 2, H, 2 * H), BF16),
            dma((7,)), dma((2,)),
            dma((2, K, 4)), dma((2, K, 4)),
            dma((2, K)), dma((2, K)),
            dma((K, NY - 1)), dma((K, NY - 1)),
            dma((K,)), dma((K,)),
            dma((Q,)), dma((Q,)),
            dma((Q, NY - 1)), dma((Q, NY - 1)),
            dma((2, 2, Q, 2)), dma((2, 2, Q, 2)),
            dma(()), dma(()),
            dma((ITERS,)), dma((ITERS,)),
            dma((ITERS,)), dma((ITERS,)),
        ],
        compiler_params=pltpu.CompilerParams(collective_id=0, has_side_effects=True),
    )(*args)
    rows = H // 2
    return pl.pallas_call(
        hand_over,
        out_shape=(
            jax.ShapeDtypeStruct((2, 8, D), BF16),
            jax.ShapeDtypeStruct((1, H, D), BF16),
        ),
        grid=(2,),
        in_specs=[
            pl.BlockSpec((2, 8, D), lambda i: (0, 0, 0)),
            pl.BlockSpec((1, rows, D), lambda i: (0, i, 0)),
        ],
        out_specs=(
            pl.BlockSpec((2, 8, D), lambda i: (0, 0, 0)),
            pl.BlockSpec((1, rows, D), lambda i: (0, i, 0)),
        ),
    )(cot, upd[None])


def solution(mesh):
    rows = P(None, ("dp", "expert", "half"), None)
    return jax.shard_map(
        on_device,
        mesh=mesh,
        in_specs=(
            rows, rows, rows, rows,
            P("expert", None, "half"), P("expert", None, "half"), P("expert", "half", None),
        ),
        out_specs=(rows, P(("dp", "expert"), "half", None)),
        check_vma=False,
    )
```

```python
import functools
import math

import jax
import jax.numpy as jnp
from jax import lax
from jax.experimental import pallas as pl
from jax.experimental.pallas import tpu as pltpu
from jax.sharding import PartitionSpec as P

MESH = pl.DeviceIdType.MESH
NY = 4
ITERS = 2
LINEAR, CUBIC, QUINTIC = 3.4445, -4.775, 2.0315
F32, BF16 = jnp.float32, jnp.bfloat16


def nt(a, b, **kw):
    return lax.dot_general(
        a, b, (((1,), (1,)), ((), ())), preferred_element_type=F32, **kw
    )


def iota(shape, axis):
    return lax.broadcasted_iota(jnp.int32, shape, axis)


def advance(gen, steps):
    for _ in range(steps):
        next(gen, None)


def kernel(
    NZ, act_hbm, ups_hbm, routes_hbm, gates_hbm, gate_hbm, up_hbm, down_hbm,
    cot_hbm, upd_hbm,
    act_ref, ups_ref, routes_ref, gates_ref, cot_ref, upd_ref, cur_ref, hid_own, hid_send, hid_in,
    zbuf, gbuf, ysend, ybuf, rows_tok, rows_sc, rows_in, gu, down,
    esend, ebuf, cbuf, rsend, rrecv,
    nsend, nrecv, whole, gram_b,
    w_sem, o_sem, z_ss, z_rs, g_ss, g_rs, y_ss, y_rs, f_ss, f_rs, p_ss, p_rs, v_ss, v_rs, e_ss, e_rs,
    r_ss, r_rs, n_ss, n_rs, x_ss, x_rs, m_ss, m_rs,
):
    K = NZ // 2
    Q = K // 2
    D = zbuf.shape[-1]
    H = hid_own.shape[-1]
    D2 = D // 2
    TN = min(512, D)
    ex = lax.axis_index("expert")
    me = lax.axis_index("half")
    z = ex // NY
    y = ex % NY
    z_up = {"expert": ((z + 1) % NZ) * NY + y}
    z_dn = {"expert": ((z + NZ - 1) % NZ) * NY + y}
    z_to = (z_up, z_dn)
    z_two = tuple({"expert": ((z + NZ + h) % NZ) * NY + y} for h in (2, -2))
    y_to = [None] + [{"expert": z * NY + (y + r) % NY} for r in range(1, NY)]
    partner = {"half": 1 - me}
    pending = []

    def send(src, dst, ss, rs, dev):
        c = pltpu.make_async_remote_copy(
            src_ref=src, dst_ref=dst, send_sem=ss, recv_sem=rs,
            device_id=dev, device_id_type=MESH,
        )
        c.start()
        pending.append(c)

    def arrived(dst, rs, dev):
        pltpu.make_async_remote_copy(
            src_ref=dst, dst_ref=dst, send_sem=rs, recv_sem=rs,
            device_id=dev, device_id_type=MESH,
        ).wait_recv()

    barrier = pltpu.get_barrier_semaphore()
    peers = [z_up, z_dn, *z_two, partner] + y_to[1:]
    for p in peers:
        pl.semaphore_signal(barrier, inc=1, device_id=p, device_id_type=MESH)

    loads = [
        pltpu.make_async_copy(src, dst, w_sem.at[n])
        for n, (src, dst) in enumerate(
            [
                (routes_hbm, routes_ref),
                (gates_hbm, gates_ref),
                (act_hbm, act_ref),
                (ups_hbm, ups_ref),
                (gate_hbm.at[0], gu.at[:, pl.ds(0, H)]),
                (up_hbm.at[0], gu.at[:, pl.ds(H, H)]),
                (down_hbm.at[0], down.at[pl.ds(0, H)]),
            ]
        )
    ]
    for c in loads:
        c.start()
    for c in loads[:4]:
        c.wait()

    lane = iota((8, 128), 1)
    sub = iota((8, 128), 0)
    for m in range(2):
        zbuf[K - 1, 0, pl.ds(m * 16, 16), :] = jnp.concatenate(
            [act_ref[m].astype(F32), ups_ref[m].astype(F32)], axis=0
        ).astype(BF16)
        route = routes_ref[m]
        gate = gates_ref[m]
        gsum = jnp.zeros((8, 128), F32)
        named = jnp.zeros((8, 128), F32)
        for k in range(route.shape[1]):
            hit = route[:, k : k + 1] == lane // 2
            gsum = gsum + jnp.where(hit, gate[:, k : k + 1], 0.0)
            named = named + jnp.where(hit, 1.0, 0.0)
        before = jnp.zeros((8, 128), F32)
        for t in range(7):
            before = before + jnp.where(sub > t, named[t : t + 1, :], 0.0)
        gbuf[K - 1, 0, pl.ds(m * 8, 8), :] = jnp.where(
            before == (lane % 2).astype(F32), gsum, 0.0
        )

    pl.semaphore_wait(barrier, len(peers))

    def hop(s, d, key):
        buf = gbuf if key == "g" else zbuf
        src = buf.at[K - 1, 0] if s == 1 else buf.at[s - 2, d]
        dst = buf.at[s - 1, d] if s < K else buf.at[K - 1, 1]
        if key == "g":
            return src, dst, g_ss.at[d, s - 1], g_rs.at[d, s - 1], z_to[d]
        m, c = key
        at = (pl.ds(m * 16, 16), pl.ds(c * D2, D2))
        ss, rs = z_ss.at[d, s - 1, 2 * m + c], z_rs.at[d, s - 1, 2 * m + c]
        return src.at[at], dst.at[at], ss, rs, z_to[d]

    def goes(s, d, key):
        return s < K or (s == K and (d == 0 if key == "g" else key[0] == d))

    halves = [(m, c) for m in range(2) for c in range(2)]
    pieces = [(d, key) for key in halves + ["g"] for d in range(2)]
    for d, key in pieces:
        send(*hop(1, d, key))

    r64, c64 = iota((64, 64), 0), iota((64, 64), 1)
    e_row, e_lane = iota((64, 128), 0), iota((64, 128), 1)
    slot_of_row = 2 * (z * NY + (y + e_row // 16) % NY) + e_row % 2
    pick = jnp.where(e_lane == slot_of_row, 1.0, 0.0)
    block_of_row = ((r64 // 4) % 2) * 4 + ((r64 // 2) % 2) * 2 + (r64 // 8) % 2
    same_block = c64 // 8 == block_of_row
    scaled_row = (iota((64, 1), 0) // 8) % 2 == 1

    def select(i):
        ga, gb = gbuf[i, 0], gbuf[i, 1]
        tokens = jnp.concatenate(
            [ga[:8], ga[:8], ga[8:], ga[8:], gb[:8], gb[:8], gb[8:], gb[8:]], axis=0
        )
        table = nt(pick, tokens, precision=lax.Precision.HIGHEST)
        table = jnp.where(same_block, table, 0.0)
        scale = jnp.where(scaled_row, jnp.sum(table, axis=1, keepdims=True), 1.0)
        chosen = jnp.where(table > 0.0, 1.0, 0.0).astype(BF16)
        for n in range(0, D, TN):
            x = zbuf[i, :, :, pl.ds(n, TN)].reshape(64, TN)
            picked = jnp.dot(chosen, x, preferred_element_type=F32) * scale
            picked = picked.astype(BF16)
            ybuf[i, 0, :, pl.ds(n, TN)] = picked[:16]
            ysend[i, :, :, pl.ds(n, TN)] = picked[16:].reshape(NY - 1, 16, TN)
        for r in range(1, NY):
            send(
                ysend.at[i, r - 1], ybuf.at[i, NY - r],
                y_ss.at[i, r - 1], y_rs.at[i, r - 1], y_to[r],
            )

    def part_rows(q):
        for i in (2 * q, 2 * q + 1):
            for r in range(1, NY):
                arrived(ybuf.at[i, NY - r], y_rs.at[i, r - 1], y_to[r])
        for r in range(NY):
            for n in range(0, D, TN):
                two = ybuf[pl.ds(2 * q, 2), r, :, pl.ds(n, TN)].astype(F32)
                at = pl.ds(r * 16, 16)
                rows_tok[q, at, pl.ds(n, TN)] = jnp.concatenate(
                    [two[0, :8], two[1, :8]], axis=0
                ).astype(BF16)
                rows_sc[q, at, pl.ds(n, TN)] = jnp.concatenate(
                    [two[0, 8:], two[1, 8:]], axis=0
                ).astype(BF16)
        send(rows_sc.at[q], rows_in.at[q], f_ss.at[q], f_rs.at[q], partner)

    def expert(q):
        tok, sc = rows_tok[q], rows_sc[q]
        boths = []
        for j in range(2):
            pre = jnp.dot(tok, gu[:, pl.ds(2 * H * j, 2 * H)], preferred_element_type=F32)
            pre_gate, pre_up = pre[:, :H], pre[:, H:]
            sig = jax.nn.sigmoid(pre_gate)
            activated = pre_gate * sig
            hidden = (activated * pre_up).astype(BF16)
            hidden_grad = nt(sc, down[pl.ds(H * j, H), :])
            gate_grad = hidden_grad * pre_up * sig * (1.0 + pre_gate * (1.0 - sig))
            boths.append(
                jnp.concatenate(
                    [gate_grad.astype(BF16), (hidden_grad * activated).astype(BF16)], axis=1
                )
            )
            if j == 0:
                hid_own[q] = hidden
            else:
                hid_send[q] = hidden
        for n in range(0, D, TN):
            at = pl.ds(n, TN)
            parts = [
                nt(boths[j], gu[at, pl.ds(2 * H * j, 2 * H)]).astype(BF16).astype(F32)
                for j in range(2)
            ]
            total = (parts[0] + parts[1]).astype(BF16)
            ebuf[q, 0, :, at] = total[:16]
            esend[q, :, :, at] = total[16:].reshape(NY - 1, 16, TN)
        for r in range(1, NY):
            send(
                esend.at[q, r - 1], ebuf.at[q, NY - r],
                e_ss.at[q, r - 1], e_rs.at[q, r - 1], y_to[r],
            )
        send(hid_send.at[q], hid_in.at[q], p_ss.at[q], p_rs.at[q], partner)

    def down_grad():
        for q in range(Q):
            arrived(rows_in.at[q], f_rs.at[q], partner)
            arrived(hid_in.at[q], p_rs.at[q], partner)
        own = hid_own[...].reshape(Q * 64, H).astype(F32).T.astype(BF16)
        taken = hid_in[...].reshape(Q * 64, H).astype(F32).T.astype(BF16)
        for n in range(0, D, TN):
            at = pl.ds(n, TN)
            grad = jnp.dot(
                own, rows_sc[:, :, at].reshape(Q * 64, TN), preferred_element_type=F32
            )
            cur_ref[:, at] = grad + jnp.dot(
                taken, rows_in[:, :, at].reshape(Q * 64, TN), preferred_element_type=F32
            )

    def combine(q):
        for r in range(1, NY):
            arrived(ebuf.at[q, NY - r], e_rs.at[q, r - 1], y_to[r])
        tokens = gbuf[pl.ds(2 * q, 2)].reshape(64, 128)
        table = nt(tokens, pick, precision=lax.Precision.HIGHEST)
        mine = (r64 // 8 == (c64 // 2) % 8) & (table > 0.0)
        chosen = jnp.where(mine, 1.0, 0.0).astype(BF16)
        for n in range(0, D, TN):
            x = ebuf[q, :, :, pl.ds(n, TN)].reshape(64, TN)
            total = jnp.dot(chosen, x, preferred_element_type=F32)
            cbuf[pl.ds(2 * q, 2), :, :, pl.ds(n, TN)] = total.reshape(2, 2, 16, TN)

    def chain(s, d, c):
        at = pl.ds(c * D2, D2)
        sem = (d, 0, s - 1, c)
        buf = (d, 0, s - 1, slice(None), at)
        return rsend.at[buf], rrecv.at[buf], r_ss.at[sem], r_rs.at[sem], z_two[d]

    def side(s, d):
        buf, sem = (d, 1, s - 1), (d, 1, s - 1, 0)
        return rsend.at[buf], rrecv.at[buf], r_ss.at[sem], r_rs.at[sem], z_to[d]

    def send_side(q):
        for d in range(2):
            rsend[d, 1, Q - q - 1] = cbuf[2 * q, 1 - d].astype(BF16)
            send(*side(Q - q, d))

    def got(copy):
        arrived(copy[1], copy[3], copy[4])

    def sum_z():
        for s in range(1, Q + 1):
            for d in range(2):
                if s > 1:
                    got(side(s - 1, d))
            for c in range(2):
                for d in range(2):
                    if s == 1 and c != d:
                        continue
                    at = pl.ds(c * D2, D2)
                    k = K + 2 - 2 * s
                    total = cbuf[k - 1, 1 if k == K else 1 - d, :, at]
                    if s > 1:
                        total = total + rrecv[d, 1, s - 2, :, at].astype(F32)
                    if s > 2 or (s == 2 and c == d):
                        got(chain(s - 1, d, c))
                        total = total + rrecv[d, 0, s - 2, :, at].astype(F32)
                    rsend[d, 0, s - 1, :, at] = total.astype(BF16)
                    send(*chain(s, d, c))
            yield
        for d in range(2):
            got(side(Q, d))
        for c in range(2):
            at = pl.ds(c * D2, D2)
            total = cbuf[K - 1, 0, :, at]
            for d in range(2):
                total = total + rrecv[d, 1, Q - 1, :, at].astype(F32)
                if Q > 1 or c == d:
                    got(chain(Q, d, c))
                    total = total + rrecv[d, 0, Q - 1, :, at].astype(F32)
            cot_ref[:, :, at] = total.reshape(2, 8, D2).astype(BF16)
        yield

    def newton():
        squares = jnp.zeros((8, 128), F32)
        for n in range(0, D, 128):
            piece = cur_ref[:, pl.ds(n, 128)]
            squares = squares + jnp.sum((piece * piece).reshape(H // 8, 8, 128), axis=0)
        nsend[...] = jnp.broadcast_to(jnp.sum(squares, keepdims=True), (8, 128))
        send(nsend, nrecv, n_ss, n_rs, partner)
        yield
        arrived(nrecv, n_rs, partner)
        norm = jnp.sqrt(nsend[...] + nrecv[...]) + 1e-07
        factor = (1.0 / norm)[:1, :1]
        for it in range(ITERS):
            mine = whole.at[it, me]
            for n in range(0, D, TN):
                at = pl.ds(n, TN)
                if it == 0:
                    value = cur_ref[:, at] * factor
                    cur_ref[:, at] = value
                    mine[:, at] = value.astype(BF16)
            send(mine, mine, x_ss.at[it], x_rs.at[it], partner)
            yield
            other = whole.at[it, 1 - me]
            gram_own = nt(mine[...], mine[...])
            yield
            arrived(other, x_rs.at[it], partner)
            gram_other = nt(mine[...], other[...])
            gm = gram_b.at[it, me]
            own_at = pl.ds(pl.multiple_of(me * H, H), H)
            other_at = pl.ds(pl.multiple_of((1 - me) * H, H), H)
            gm[:, own_at] = gram_own.astype(BF16)
            gm[:, other_at] = gram_other.astype(BF16)
            send(gm, gm, m_ss.at[it], m_rs.at[it], partner)
            yield
            arrived(gram_b.at[it, 1 - me], m_rs.at[it], partner)
            full = gram_b[it].reshape(2 * H, 2 * H)
            square = jnp.dot(gm[...], full, preferred_element_type=F32)
            sq_own = jnp.where(me == 0, square[:, :H], square[:, H:])
            sq_other = jnp.where(me == 0, square[:, H:], square[:, :H])
            p_own = (CUBIC * gram_own + QUINTIC * sq_own).astype(BF16)
            p_other = (CUBIC * gram_other + QUINTIC * sq_other).astype(BF16)
            yield
            for n in range(0, D, TN):
                at = pl.ds(n, TN)
                step = jnp.dot(p_own, mine[:, at], preferred_element_type=F32)
                step = step + jnp.dot(p_other, other[:, at], preferred_element_type=F32)
                value = LINEAR * cur_ref[:, at] + step
                if it + 1 < ITERS:
                    cur_ref[:, at] = value
                    whole.at[it + 1, me][:, at] = value.astype(BF16)
                else:
                    upd_ref[:, at] = (value * math.sqrt(max(2 * H, D))).astype(BF16)
            yield
        pltpu.make_async_copy(upd_ref, upd_hbm, o_sem.at[0]).start()

    shares = [
        (gate_hbm.at[0], gu.at[:, pl.ds(2 * H, H)]),
        (up_hbm.at[0], gu.at[:, pl.ds(3 * H, H)]),
        (down_hbm.at[0], down.at[pl.ds(H, H)]),
    ]
    for n, (src, dst) in enumerate(shares):
        send(src, dst, v_ss.at[n], v_rs.at[n], partner)

    done = 0
    for s in range(1, K + 1):
        for d, key in pieces:
            if goes(s, d, key):
                arrived(*hop(s, d, key)[1::2], z_to[d])
                if goes(s + 1, d, key):
                    send(*hop(s + 1, d, key))
        select(s - 1)
        if s == K - 2 or (s == K and K < 3):
            for c in loads[4:]:
                c.wait()
            for n, (_, dst) in enumerate(shares):
                arrived(dst, v_rs.at[n], partner)
        if s >= K - 2 and 2 * done + 3 < s:
            part_rows(done)
            expert(done)
            done += 1
    for q in range(done, Q):
        part_rows(q)
        expert(q)
    for q in range(Q - 2):
        combine(q)
        send_side(q)
    down_grad()
    ns = newton()
    advance(ns, 1)
    combine(Q - 1)
    ring = sum_z()
    advance(ring, 1)
    send_side(Q - 1)
    if Q > 1:
        combine(Q - 2)
        send_side(Q - 2)
    for s in range(2, Q + 1):
        advance(ns, 3)
        advance(ring, 1)
    advance(ns, 20)
    advance(ring, 2)
    cot_out = pltpu.make_async_copy(cot_ref, cot_hbm, o_sem.at[1])
    cot_out.start()
    for c in pending:
        c.wait_send()
    cot_out.wait()
    pltpu.make_async_copy(upd_ref, upd_hbm, o_sem.at[0]).wait()


def hand_over(cot_ref, upd_ref, cot_out, upd_out):
    cot_out[...] = cot_ref[...]
    upd_out[...] = upd_ref[...]


def on_device(activations, upstream, routes, route_gates, gate_matrix, up_matrix, down_matrix):
    NZ = lax.axis_size("expert") // NY
    K = NZ // 2
    Q = K // 2
    D = activations.shape[2]
    H = down_matrix.shape[1]
    dma = pltpu.SemaphoreType.DMA
    anywhere = pl.BlockSpec(memory_space=pl.ANY)
    args = (activations, upstream, routes, route_gates, gate_matrix, up_matrix, down_matrix)
    cot, upd = pl.pallas_call(
        functools.partial(kernel, NZ),
        out_shape=(
            jax.ShapeDtypeStruct((2, 8, D), BF16),
            jax.ShapeDtypeStruct((H, D), BF16),
        ),
        in_specs=[anywhere] * 7,
        out_specs=(anywhere, anywhere),
        scratch_shapes=[
            pltpu.VMEM(activations.shape, BF16),
            pltpu.VMEM(upstream.shape, BF16),
            pltpu.VMEM(routes.shape, routes.dtype),
            pltpu.VMEM(route_gates.shape, F32),
            pltpu.VMEM((2, 8, D), BF16),
            pltpu.VMEM((H, D), BF16),
            pltpu.VMEM((H, D), F32),
            pltpu.VMEM((Q, 64, H), BF16),
            pltpu.VMEM((Q, 64, H), BF16),
            pltpu.VMEM((Q, 64, H), BF16),
            pltpu.VMEM((K, 2, 32, D), BF16),
            pltpu.VMEM((K, 2, 16, 128), F32),
            pltpu.VMEM((K, NY - 1, 16, D), BF16),
            pltpu.VMEM((K, NY, 16, D), BF16),
            pltpu.VMEM((Q, 64, D), BF16),
            pltpu.VMEM((Q, 64, D), BF16),
            pltpu.VMEM((Q, 64, D), BF16),
            pltpu.VMEM((D, 4 * H), BF16),
            pltpu.VMEM((2 * H, D), BF16),
            pltpu.VMEM((Q, NY - 1, 16, D), BF16),
            pltpu.VMEM((Q, NY, 16, D), BF16),
            pltpu.VMEM((K, 2, 16, D), F32),
            pltpu.VMEM((2, 2, Q, 16, D), BF16),
            pltpu.VMEM((2, 2, Q, 16, D), BF16),
            pltpu.VMEM((8, 128), F32),
            pltpu.VMEM((8, 128), F32),
            pltpu.VMEM((ITERS, 2, H, D), BF16),
            pltpu.VMEM((ITERS, 2, H, 2 * H), BF16),
            dma((7,)), dma((2,)),
            dma((2, K, 4)), dma((2, K, 4)),
            dma((2, K)), dma((2, K)),
            dma((K, NY - 1)), dma((K, NY - 1)),
            dma((Q,)), dma((Q,)),
            dma((Q,)), dma((Q,)),
            dma((3,)), dma((3,)),
            dma((Q, NY - 1)), dma((Q, NY - 1)),
            dma((2, 2, Q, 2)), dma((2, 2, Q, 2)),
            dma(()), dma(()),
            dma((ITERS,)), dma((ITERS,)),
            dma((ITERS,)), dma((ITERS,)),
        ],
        compiler_params=pltpu.CompilerParams(collective_id=0, has_side_effects=True),
    )(*args)
    rows = H // 2
    return pl.pallas_call(
        hand_over,
        out_shape=(
            jax.ShapeDtypeStruct((2, 8, D), BF16),
            jax.ShapeDtypeStruct((1, H, D), BF16),
        ),
        grid=(2,),
        in_specs=[
            pl.BlockSpec((2, 8, D), lambda i: (0, 0, 0)),
            pl.BlockSpec((1, rows, D), lambda i: (0, i, 0)),
        ],
        out_specs=(
            pl.BlockSpec((2, 8, D), lambda i: (0, 0, 0)),
            pl.BlockSpec((1, rows, D), lambda i: (0, i, 0)),
        ),
    )(cot, upd[None])


def solution(mesh):
    rows = P(None, ("dp", "expert", "half"), None)
    return jax.shard_map(
        on_device,
        mesh=mesh,
        in_specs=(
            rows, rows, rows, rows,
            P("expert", None, "half"), P("expert", None, "half"), P("expert", "half", None),
        ),
        out_specs=(rows, P(("dp", "expert"), "half", None)),
        check_vma=False,
    )
```

```python
import functools
import math

import jax
import jax.numpy as jnp
from jax import lax
from jax.experimental import pallas as pl
from jax.experimental.pallas import tpu as pltpu
from jax.sharding import PartitionSpec as P

MESH = pl.DeviceIdType.MESH
NY = 4
ITERS = 2
LINEAR, CUBIC, QUINTIC = 3.4445, -4.775, 2.0315
F32, BF16 = jnp.float32, jnp.bfloat16


def nt(a, b, **kw):
    return lax.dot_general(
        a, b, (((1,), (1,)), ((), ())), preferred_element_type=F32, **kw
    )


def iota(shape, axis):
    return lax.broadcasted_iota(jnp.int32, shape, axis)


def advance(gen, steps):
    for _ in range(steps):
        next(gen, None)


def kernel(
    NZ, act_hbm, ups_hbm, routes_hbm, gates_hbm, gate_hbm, up_hbm, down_hbm,
    cot_hbm, upd_hbm,
    act_ref, ups_ref, routes_ref, gates_ref, cot_ref, upd_ref, cur_ref, hid_own, hid_send, hid_in, both,
    zbuf, gbuf, ysend, ybuf, rows_tok, rows_sc, rows_in, gu, down,
    esend, ebuf, cbuf, rsend, rrecv,
    nsend, nrecv, whole, gram_b,
    w_sem, o_sem, z_ss, z_rs, g_ss, g_rs, y_ss, y_rs, f_ss, f_rs, p_ss, p_rs, v_ss, v_rs, e_ss, e_rs,
    r_ss, r_rs, n_ss, n_rs, x_ss, x_rs, m_ss, m_rs,
):
    K = NZ // 2
    Q = K // 2
    D = zbuf.shape[-1]
    H = hid_own.shape[-1]
    D2 = D // 2
    TN = min(512, D)
    ex = lax.axis_index("expert")
    me = lax.axis_index("half")
    z = ex // NY
    y = ex % NY
    z_up = {"expert": ((z + 1) % NZ) * NY + y}
    z_dn = {"expert": ((z + NZ - 1) % NZ) * NY + y}
    z_to = (z_up, z_dn)
    z_two = tuple({"expert": ((z + NZ + h) % NZ) * NY + y} for h in (2, -2))
    y_to = [None] + [{"expert": z * NY + (y + r) % NY} for r in range(1, NY)]
    partner = {"half": 1 - me}
    pending = []

    def send(src, dst, ss, rs, dev):
        c = pltpu.make_async_remote_copy(
            src_ref=src, dst_ref=dst, send_sem=ss, recv_sem=rs,
            device_id=dev, device_id_type=MESH,
        )
        c.start()
        pending.append(c)

    def arrived(dst, rs, dev):
        pltpu.make_async_remote_copy(
            src_ref=dst, dst_ref=dst, send_sem=rs, recv_sem=rs,
            device_id=dev, device_id_type=MESH,
        ).wait_recv()

    barrier = pltpu.get_barrier_semaphore()
    peers = [z_up, z_dn, *z_two, partner] + y_to[1:]
    for p in peers:
        pl.semaphore_signal(barrier, inc=1, device_id=p, device_id_type=MESH)

    loads = [
        pltpu.make_async_copy(src, dst, w_sem.at[n])
        for n, (src, dst) in enumerate(
            [
                (routes_hbm, routes_ref),
                (gates_hbm, gates_ref),
                (act_hbm, act_ref),
                (ups_hbm, ups_ref),
                (gate_hbm.at[0], gu.at[:, pl.ds(0, H)]),
                (up_hbm.at[0], gu.at[:, pl.ds(H, H)]),
                (down_hbm.at[0], down.at[pl.ds(0, H)]),
            ]
        )
    ]
    for c in loads:
        c.start()
    for c in loads[:4]:
        c.wait()

    lane = iota((8, 128), 1)
    sub = iota((8, 128), 0)
    for m in range(2):
        zbuf[K - 1, 0, pl.ds(m * 16, 16), :] = jnp.concatenate(
            [act_ref[m].astype(F32), ups_ref[m].astype(F32)], axis=0
        ).astype(BF16)
        route = routes_ref[m]
        gate = gates_ref[m]
        gsum = jnp.zeros((8, 128), F32)
        named = jnp.zeros((8, 128), F32)
        for k in range(route.shape[1]):
            hit = route[:, k : k + 1] == lane // 2
            gsum = gsum + jnp.where(hit, gate[:, k : k + 1], 0.0)
            named = named + jnp.where(hit, 1.0, 0.0)
        before = jnp.zeros((8, 128), F32)
        for t in range(7):
            before = before + jnp.where(sub > t, named[t : t + 1, :], 0.0)
        gbuf[K - 1, 0, pl.ds(m * 8, 8), :] = jnp.where(
            before == (lane % 2).astype(F32), gsum, 0.0
        )

    pl.semaphore_wait(barrier, len(peers))

    def hop(s, d, key):
        buf = gbuf if key == "g" else zbuf
        src = buf.at[K - 1, 0] if s == 1 else buf.at[s - 2, d]
        dst = buf.at[s - 1, d] if s < K else buf.at[K - 1, 1]
        if key == "g":
            return src, dst, g_ss.at[d, s - 1], g_rs.at[d, s - 1], z_to[d]
        m, c = key
        at = (pl.ds(m * 16, 16), pl.ds(c * D2, D2))
        ss, rs = z_ss.at[d, s - 1, 2 * m + c], z_rs.at[d, s - 1, 2 * m + c]
        return src.at[at], dst.at[at], ss, rs, z_to[d]

    def goes(s, d, key):
        return s < K or (s == K and (d == 0 if key == "g" else key[0] == d))

    halves = [(m, c) for m in range(2) for c in range(2)]
    pieces = [(d, key) for key in halves + ["g"] for d in range(2)]
    for d, key in pieces:
        send(*hop(1, d, key))

    r64, c64 = iota((64, 64), 0), iota((64, 64), 1)
    e_row, e_lane = iota((64, 128), 0), iota((64, 128), 1)
    slot_of_row = 2 * (z * NY + (y + e_row // 16) % NY) + e_row % 2
    pick = jnp.where(e_lane == slot_of_row, 1.0, 0.0)
    block_of_row = ((r64 // 4) % 2) * 4 + ((r64 // 2) % 2) * 2 + (r64 // 8) % 2
    same_block = c64 // 8 == block_of_row
    scaled_row = (iota((64, 1), 0) // 8) % 2 == 1

    def select(i):
        ga, gb = gbuf[i, 0], gbuf[i, 1]
        tokens = jnp.concatenate(
            [ga[:8], ga[:8], ga[8:], ga[8:], gb[:8], gb[:8], gb[8:], gb[8:]], axis=0
        )
        table = nt(pick, tokens, precision=lax.Precision.HIGHEST)
        table = jnp.where(same_block, table, 0.0)
        scale = jnp.where(scaled_row, jnp.sum(table, axis=1, keepdims=True), 1.0)
        chosen = jnp.where(table > 0.0, 1.0, 0.0).astype(BF16)
        for n in range(0, D, TN):
            x = zbuf[i, :, :, pl.ds(n, TN)].reshape(64, TN)
            picked = jnp.dot(chosen, x, preferred_element_type=F32) * scale
            picked = picked.astype(BF16)
            ybuf[i, 0, :, pl.ds(n, TN)] = picked[:16]
            ysend[i, :, :, pl.ds(n, TN)] = picked[16:].reshape(NY - 1, 16, TN)
        for r in range(1, NY):
            send(
                ysend.at[i, r - 1], ybuf.at[i, NY - r],
                y_ss.at[i, r - 1], y_rs.at[i, r - 1], y_to[r],
            )

    def part_rows(q):
        for i in (2 * q, 2 * q + 1):
            for r in range(1, NY):
                arrived(ybuf.at[i, NY - r], y_rs.at[i, r - 1], y_to[r])
        for r in range(NY):
            for n in range(0, D, TN):
                two = ybuf[pl.ds(2 * q, 2), r, :, pl.ds(n, TN)].astype(F32)
                at = pl.ds(r * 16, 16)
                rows_tok[q, at, pl.ds(n, TN)] = jnp.concatenate(
                    [two[0, :8], two[1, :8]], axis=0
                ).astype(BF16)
                rows_sc[q, at, pl.ds(n, TN)] = jnp.concatenate(
                    [two[0, 8:], two[1, 8:]], axis=0
                ).astype(BF16)
        send(rows_sc.at[q], rows_in.at[q], f_ss.at[q], f_rs.at[q], partner)

    def expert(q, nq):
        rows = nq * 64
        at_q = pl.ds(q, nq)
        for j in range(2):
            tok = rows_tok[at_q].reshape(rows, D)
            pre = jnp.dot(tok, gu[:, pl.ds(2 * H * j, 2 * H)], preferred_element_type=F32)
            pre_gate, pre_up = pre[:, :H], pre[:, H:]
            sig = jax.nn.sigmoid(pre_gate)
            activated = pre_gate * sig
            hidden = (activated * pre_up).astype(BF16)
            hidden_grad = nt(rows_sc[at_q].reshape(rows, D), down[pl.ds(H * j, H), :])
            gate_grad = hidden_grad * pre_up * sig * (1.0 + pre_gate * (1.0 - sig))
            both[j, pl.ds(0, rows), pl.ds(0, H)] = gate_grad.astype(BF16)
            both[j, pl.ds(0, rows), pl.ds(H, H)] = (hidden_grad * activated).astype(BF16)
            if j == 0:
                hid_own[at_q] = hidden.reshape(nq, 64, H)
            else:
                hid_send[at_q] = hidden.reshape(nq, 64, H)
            yield
        for n in range(0, D, TN):
            at = pl.ds(n, TN)
            parts = [
                nt(both[j, pl.ds(0, rows)], gu[at, pl.ds(2 * H * j, 2 * H)])
                for j in range(2)
            ]
            parts = [p.astype(BF16).astype(F32) for p in parts]
            total = (parts[0] + parts[1]).astype(BF16).reshape(nq, 64, TN)
            ebuf[at_q, 0, :, at] = total[:, :16]
            esend[at_q, :, :, at] = total[:, 16:].reshape(nq, NY - 1, 16, TN)
        for p in range(q, q + nq):
            for r in (2, 1, 3):
                send(
                    esend.at[p, r - 1], ebuf.at[p, NY - r],
                    e_ss.at[p, r - 1], e_rs.at[p, r - 1], y_to[r],
                )
            send(hid_send.at[p], hid_in.at[p], p_ss.at[p], p_rs.at[p], partner)
        yield

    def down_grad():
        for q in range(Q):
            arrived(rows_in.at[q], f_rs.at[q], partner)
            arrived(hid_in.at[q], p_rs.at[q], partner)
        own = hid_own[...].reshape(Q * 64, H).astype(F32).T.astype(BF16)
        taken = hid_in[...].reshape(Q * 64, H).astype(F32).T.astype(BF16)
        for n in range(0, D, TN):
            at = pl.ds(n, TN)
            grad = jnp.dot(
                own, rows_sc[:, :, at].reshape(Q * 64, TN), preferred_element_type=F32
            )
            cur_ref[:, at] = grad + jnp.dot(
                taken, rows_in[:, :, at].reshape(Q * 64, TN), preferred_element_type=F32
            )

    def combine(q):
        for r in range(1, NY):
            arrived(ebuf.at[q, NY - r], e_rs.at[q, r - 1], y_to[r])
        tokens = gbuf[pl.ds(2 * q, 2)].reshape(64, 128)
        table = nt(tokens, pick, precision=lax.Precision.HIGHEST)
        mine = (r64 // 8 == (c64 // 2) % 8) & (table > 0.0)
        chosen = jnp.where(mine, 1.0, 0.0).astype(BF16)
        for n in range(0, D, TN):
            x = ebuf[q, :, :, pl.ds(n, TN)].reshape(64, TN)
            total = jnp.dot(chosen, x, preferred_element_type=F32)
            cbuf[pl.ds(2 * q, 2), :, :, pl.ds(n, TN)] = total.reshape(2, 2, 16, TN)

    def chain(s, d, c):
        at = pl.ds(c * D2, D2)
        sem = (d, 0, s - 1, c)
        buf = (d, 0, s - 1, slice(None), at)
        return rsend.at[buf], rrecv.at[buf], r_ss.at[sem], r_rs.at[sem], z_two[d]

    def side(s, d):
        buf, sem = (d, 1, s - 1), (d, 1, s - 1, 0)
        return rsend.at[buf], rrecv.at[buf], r_ss.at[sem], r_rs.at[sem], z_to[d]

    def send_side(q):
        for d in range(2):
            rsend[d, 1, Q - q - 1] = cbuf[2 * q, 1 - d].astype(BF16)
            send(*side(Q - q, d))

    def got(copy):
        arrived(copy[1], copy[3], copy[4])

    def sum_z():
        for s in range(1, Q + 1):
            for d in range(2):
                if s > 1:
                    got(side(s - 1, d))
            for c in range(2):
                for d in range(2):
                    if s == 1 and c != d:
                        continue
                    at = pl.ds(c * D2, D2)
                    k = K + 2 - 2 * s
                    total = cbuf[k - 1, 1 if k == K else 1 - d, :, at]
                    if s > 1:
                        total = total + rrecv[d, 1, s - 2, :, at].astype(F32)
                    if s > 2 or (s == 2 and c == d):
                        got(chain(s - 1, d, c))
                        total = total + rrecv[d, 0, s - 2, :, at].astype(F32)
                    rsend[d, 0, s - 1, :, at] = total.astype(BF16)
                    send(*chain(s, d, c))
            yield
        for d in range(2):
            got(side(Q, d))
        for c in range(2):
            at = pl.ds(c * D2, D2)
            total = cbuf[K - 1, 0, :, at]
            for d in range(2):
                total = total + rrecv[d, 1, Q - 1, :, at].astype(F32)
                if Q > 1 or c == d:
                    got(chain(Q, d, c))
                    total = total + rrecv[d, 0, Q - 1, :, at].astype(F32)
            cot_ref[:, :, at] = total.reshape(2, 8, D2).astype(BF16)
        yield

    def newton():
        squares = jnp.zeros((8, 128), F32)
        for n in range(0, D, 128):
            piece = cur_ref[:, pl.ds(n, 128)]
            squares = squares + jnp.sum((piece * piece).reshape(H // 8, 8, 128), axis=0)
        nsend[...] = jnp.broadcast_to(jnp.sum(squares, keepdims=True), (8, 128))
        send(nsend, nrecv, n_ss, n_rs, partner)
        yield
        arrived(nrecv, n_rs, partner)
        norm = jnp.sqrt(nsend[...] + nrecv[...]) + 1e-07
        factor = (1.0 / norm)[:1, :1]
        for it in range(ITERS):
            mine = whole.at[it, me]
            for n in range(0, D, TN):
                at = pl.ds(n, TN)
                if it == 0:
                    value = cur_ref[:, at] * factor
                    cur_ref[:, at] = value
                    mine[:, at] = value.astype(BF16)
            send(mine, mine, x_ss.at[it], x_rs.at[it], partner)
            yield
            other = whole.at[it, 1 - me]
            gram_own = nt(mine[...], mine[...])
            yield
            arrived(other, x_rs.at[it], partner)
            gram_other = nt(mine[...], other[...])
            gm = gram_b.at[it, me]
            own_at = pl.ds(pl.multiple_of(me * H, H), H)
            other_at = pl.ds(pl.multiple_of((1 - me) * H, H), H)
            gm[:, own_at] = gram_own.astype(BF16)
            gm[:, other_at] = gram_other.astype(BF16)
            send(gm, gm, m_ss.at[it], m_rs.at[it], partner)
            yield
            arrived(gram_b.at[it, 1 - me], m_rs.at[it], partner)
            full = gram_b[it].reshape(2 * H, 2 * H)
            square = jnp.dot(gm[...], full, preferred_element_type=F32)
            sq_own = jnp.where(me == 0, square[:, :H], square[:, H:])
            sq_other = jnp.where(me == 0, square[:, H:], square[:, :H])
            p_own = (CUBIC * gram_own + QUINTIC * sq_own).astype(BF16)
            p_other = (CUBIC * gram_other + QUINTIC * sq_other).astype(BF16)
            yield
            for n in range(0, D, TN):
                at = pl.ds(n, TN)
                step = jnp.dot(p_own, mine[:, at], preferred_element_type=F32)
                step = step + jnp.dot(p_other, other[:, at], preferred_element_type=F32)
                value = LINEAR * cur_ref[:, at] + step
                if it + 1 < ITERS:
                    cur_ref[:, at] = value
                    whole.at[it + 1, me][:, at] = value.astype(BF16)
                else:
                    upd_ref[:, at] = (value * math.sqrt(max(2 * H, D))).astype(BF16)
            yield
        pltpu.make_async_copy(upd_ref, upd_hbm, o_sem.at[0]).start()

    shares = [
        (gate_hbm.at[0], gu.at[:, pl.ds(2 * H, H)]),
        (up_hbm.at[0], gu.at[:, pl.ds(3 * H, H)]),
        (down_hbm.at[0], down.at[pl.ds(H, H)]),
    ]
    for n, (src, dst) in enumerate(shares):
        send(src, dst, v_ss.at[n], v_rs.at[n], partner)

    def weights_here():
        for c in loads[4:]:
            c.wait()
        for n, (_, dst) in enumerate(shares):
            arrived(dst, v_rs.at[n], partner)

    early = max(0, Q - 2)
    first = iter(())
    for s in range(1, K + 1):
        for d, key in pieces:
            if goes(s, d, key):
                arrived(*hop(s, d, key)[1::2], z_to[d])
                if goes(s + 1, d, key):
                    send(*hop(s + 1, d, key))
        select(s - 1)
        if early and s == K - 2:
            weights_here()
            for q in range(early):
                part_rows(q)
            first = expert(0, early)
        advance(first, 1)
    advance(first, 3)
    if not early:
        weights_here()
    for q in range(early, Q):
        part_rows(q)
        advance(expert(q, 1), 3)
    for q in range(Q - 2):
        combine(q)
        send_side(q)
    down_grad()
    ns = newton()
    advance(ns, 1)
    combine(Q - 1)
    ring = sum_z()
    advance(ring, 1)
    send_side(Q - 1)
    if Q > 1:
        combine(Q - 2)
        send_side(Q - 2)
    for s in range(2, Q + 1):
        advance(ns, 3)
        advance(ring, 1)
    advance(ns, 20)
    advance(ring, 2)
    cot_out = pltpu.make_async_copy(cot_ref, cot_hbm, o_sem.at[1])
    cot_out.start()
    for c in pending:
        c.wait_send()
    cot_out.wait()
    pltpu.make_async_copy(upd_ref, upd_hbm, o_sem.at[0]).wait()


def hand_over(cot_ref, upd_ref, cot_out, upd_out):
    cot_out[...] = cot_ref[...]
    upd_out[...] = upd_ref[...]


def on_device(activations, upstream, routes, route_gates, gate_matrix, up_matrix, down_matrix):
    NZ = lax.axis_size("expert") // NY
    K = NZ // 2
    Q = K // 2
    D = activations.shape[2]
    H = down_matrix.shape[1]
    dma = pltpu.SemaphoreType.DMA
    anywhere = pl.BlockSpec(memory_space=pl.ANY)
    args = (activations, upstream, routes, route_gates, gate_matrix, up_matrix, down_matrix)
    cot, upd = pl.pallas_call(
        functools.partial(kernel, NZ),
        out_shape=(
            jax.ShapeDtypeStruct((2, 8, D), BF16),
            jax.ShapeDtypeStruct((H, D), BF16),
        ),
        in_specs=[anywhere] * 7,
        out_specs=(anywhere, anywhere),
        scratch_shapes=[
            pltpu.VMEM(activations.shape, BF16),
            pltpu.VMEM(upstream.shape, BF16),
            pltpu.VMEM(routes.shape, routes.dtype),
            pltpu.VMEM(route_gates.shape, F32),
            pltpu.VMEM((2, 8, D), BF16),
            pltpu.VMEM((H, D), BF16),
            pltpu.VMEM((H, D), F32),
            pltpu.VMEM((Q, 64, H), BF16),
            pltpu.VMEM((Q, 64, H), BF16),
            pltpu.VMEM((Q, 64, H), BF16),
            pltpu.VMEM((2, max(1, Q - 2) * 64, 2 * H), BF16),
            pltpu.VMEM((K, 2, 32, D), BF16),
            pltpu.VMEM((K, 2, 16, 128), F32),
            pltpu.VMEM((K, NY - 1, 16, D), BF16),
            pltpu.VMEM((K, NY, 16, D), BF16),
            pltpu.VMEM((Q, 64, D), BF16),
            pltpu.VMEM((Q, 64, D), BF16),
            pltpu.VMEM((Q, 64, D), BF16),
            pltpu.VMEM((D, 4 * H), BF16),
            pltpu.VMEM((2 * H, D), BF16),
            pltpu.VMEM((Q, NY - 1, 16, D), BF16),
            pltpu.VMEM((Q, NY, 16, D), BF16),
            pltpu.VMEM((K, 2, 16, D), F32),
            pltpu.VMEM((2, 2, Q, 16, D), BF16),
            pltpu.VMEM((2, 2, Q, 16, D), BF16),
            pltpu.VMEM((8, 128), F32),
            pltpu.VMEM((8, 128), F32),
            pltpu.VMEM((ITERS, 2, H, D), BF16),
            pltpu.VMEM((ITERS, 2, H, 2 * H), BF16),
            dma((7,)), dma((2,)),
            dma((2, K, 4)), dma((2, K, 4)),
            dma((2, K)), dma((2, K)),
            dma((K, NY - 1)), dma((K, NY - 1)),
            dma((Q,)), dma((Q,)),
            dma((Q,)), dma((Q,)),
            dma((3,)), dma((3,)),
            dma((Q, NY - 1)), dma((Q, NY - 1)),
            dma((2, 2, Q, 2)), dma((2, 2, Q, 2)),
            dma(()), dma(()),
            dma((ITERS,)), dma((ITERS,)),
            dma((ITERS,)), dma((ITERS,)),
        ],
        compiler_params=pltpu.CompilerParams(collective_id=0, has_side_effects=True),
    )(*args)
    rows = H // 2
    return pl.pallas_call(
        hand_over,
        out_shape=(
            jax.ShapeDtypeStruct((2, 8, D), BF16),
            jax.ShapeDtypeStruct((1, H, D), BF16),
        ),
        grid=(2,),
        in_specs=[
            pl.BlockSpec((2, 8, D), lambda i: (0, 0, 0)),
            pl.BlockSpec((1, rows, D), lambda i: (0, i, 0)),
        ],
        out_specs=(
            pl.BlockSpec((2, 8, D), lambda i: (0, 0, 0)),
            pl.BlockSpec((1, rows, D), lambda i: (0, i, 0)),
        ),
    )(cot, upd[None])


def solution(mesh):
    rows = P(None, ("dp", "expert", "half"), None)
    return jax.shard_map(
        on_device,
        mesh=mesh,
        in_specs=(
            rows, rows, rows, rows,
            P("expert", None, "half"), P("expert", None, "half"), P("expert", "half", None),
        ),
        out_specs=(rows, P(("dp", "expert"), "half", None)),
        check_vma=False,
    )
```

```python
import functools
import math

import jax
import jax.numpy as jnp
from jax import lax
from jax.experimental import pallas as pl
from jax.experimental.pallas import tpu as pltpu
from jax.sharding import PartitionSpec as P

MESH = pl.DeviceIdType.MESH
NY = 4
ITERS = 2
LINEAR, CUBIC, QUINTIC = 3.4445, -4.775, 2.0315
F32, BF16 = jnp.float32, jnp.bfloat16


def nt(a, b, **kw):
    return lax.dot_general(
        a, b, (((1,), (1,)), ((), ())), preferred_element_type=F32, **kw
    )


def iota(shape, axis):
    return lax.broadcasted_iota(jnp.int32, shape, axis)


def advance(gen, steps):
    for _ in range(steps):
        next(gen, None)


def kernel(
    NZ, act_hbm, ups_hbm, routes_hbm, gates_hbm, gate_hbm, up_hbm, down_hbm,
    cot_hbm, upd_hbm,
    act_ref, ups_ref, routes_ref, gates_ref, cot_ref, upd_ref, cur_ref, hid_own, hid_send, hid_in, both,
    zbuf, gbuf, ysend, ybuf, rows_tok, rows_sc, rows_in, gu, down,
    esend, ebuf, cbuf, rsend, rrecv,
    nsend, nrecv, whole, gram_b,
    w_sem, o_sem, z_ss, z_rs, g_ss, g_rs, y_ss, y_rs, f_ss, f_rs, p_ss, p_rs, v_ss, v_rs, e_ss, e_rs,
    r_ss, r_rs, n_ss, n_rs, x_ss, x_rs, m_ss, m_rs,
):
    K = NZ // 2
    Q = K // 2
    D = zbuf.shape[-1]
    H = hid_own.shape[-1]
    D2 = D // 2
    TN = min(512, D)
    ex = lax.axis_index("expert")
    me = lax.axis_index("half")
    z = ex // NY
    y = ex % NY
    z_up = {"expert": ((z + 1) % NZ) * NY + y}
    z_dn = {"expert": ((z + NZ - 1) % NZ) * NY + y}
    z_to = (z_up, z_dn)
    z_two = tuple({"expert": ((z + NZ + h) % NZ) * NY + y} for h in (2, -2))
    y_to = [None] + [{"expert": z * NY + (y + r) % NY} for r in range(1, NY)]
    partner = {"half": 1 - me}
    pending = []

    def send(src, dst, ss, rs, dev):
        c = pltpu.make_async_remote_copy(
            src_ref=src, dst_ref=dst, send_sem=ss, recv_sem=rs,
            device_id=dev, device_id_type=MESH,
        )
        c.start()
        pending.append(c)

    def arrived(dst, rs, dev):
        pltpu.make_async_remote_copy(
            src_ref=dst, dst_ref=dst, send_sem=rs, recv_sem=rs,
            device_id=dev, device_id_type=MESH,
        ).wait_recv()

    barrier = pltpu.get_barrier_semaphore()
    peers = [z_up, z_dn, *z_two, partner] + y_to[1:]
    for p in peers:
        pl.semaphore_signal(barrier, inc=1, device_id=p, device_id_type=MESH)

    loads = [
        pltpu.make_async_copy(src, dst, w_sem.at[n])
        for n, (src, dst) in enumerate(
            [
                (routes_hbm, routes_ref),
                (gates_hbm, gates_ref),
                (act_hbm, act_ref),
                (ups_hbm, ups_ref),
                (gate_hbm.at[0], gu.at[:, pl.ds(0, H)]),
                (up_hbm.at[0], gu.at[:, pl.ds(H, H)]),
                (down_hbm.at[0], down.at[pl.ds(0, H)]),
            ]
        )
    ]
    for c in loads:
        c.start()
    for c in loads[:4]:
        c.wait()

    lane = iota((8, 128), 1)
    sub = iota((8, 128), 0)
    for m in range(2):
        zbuf[K - 1, 0, pl.ds(m * 16, 16), :] = jnp.concatenate(
            [act_ref[m].astype(F32), ups_ref[m].astype(F32)], axis=0
        ).astype(BF16)
        route = routes_ref[m]
        gate = gates_ref[m]
        gsum = jnp.zeros((8, 128), F32)
        named = jnp.zeros((8, 128), F32)
        for k in range(route.shape[1]):
            hit = route[:, k : k + 1] == lane // 2
            gsum = gsum + jnp.where(hit, gate[:, k : k + 1], 0.0)
            named = named + jnp.where(hit, 1.0, 0.0)
        before = jnp.zeros((8, 128), F32)
        for t in range(7):
            before = before + jnp.where(sub > t, named[t : t + 1, :], 0.0)
        gbuf[K - 1, 0, pl.ds(m * 8, 8), :] = jnp.where(
            before == (lane % 2).astype(F32), gsum, 0.0
        )

    pl.semaphore_wait(barrier, len(peers))

    def hop(s, d, key):
        buf = gbuf if key == "g" else zbuf
        src = buf.at[K - 1, 0] if s == 1 else buf.at[s - 2, d]
        dst = buf.at[s - 1, d] if s < K else buf.at[K - 1, 1]
        if key == "g":
            return src, dst, g_ss.at[d, s - 1], g_rs.at[d, s - 1], z_to[d]
        m, c = key
        at = (pl.ds(m * 16, 16), pl.ds(c * D2, D2))
        ss, rs = z_ss.at[d, s - 1, 2 * m + c], z_rs.at[d, s - 1, 2 * m + c]
        return src.at[at], dst.at[at], ss, rs, z_to[d]

    def goes(s, d, key):
        return s < K or (s == K and (d == 0 if key == "g" else key[0] == d))

    halves = [(m, c) for m in range(2) for c in range(2)]
    pieces = [(d, key) for key in halves + ["g"] for d in range(2)]
    for d, key in pieces:
        send(*hop(1, d, key))

    r64, c64 = iota((64, 64), 0), iota((64, 64), 1)
    e_row, e_lane = iota((64, 128), 0), iota((64, 128), 1)
    slot_of_row = 2 * (z * NY + (y + e_row // 16) % NY) + e_row % 2
    pick = jnp.where(e_lane == slot_of_row, 1.0, 0.0)
    block_of_row = ((r64 // 4) % 2) * 4 + ((r64 // 2) % 2) * 2 + (r64 // 8) % 2
    same_block = c64 // 8 == block_of_row
    scaled_row = (iota((64, 1), 0) // 8) % 2 == 1

    def select(i):
        ga, gb = gbuf[i, 0], gbuf[i, 1]
        tokens = jnp.concatenate(
            [ga[:8], ga[:8], ga[8:], ga[8:], gb[:8], gb[:8], gb[8:], gb[8:]], axis=0
        )
        table = nt(pick, tokens, precision=lax.Precision.HIGHEST)
        table = jnp.where(same_block, table, 0.0)
        scale = jnp.where(scaled_row, jnp.sum(table, axis=1, keepdims=True), 1.0)
        chosen = jnp.where(table > 0.0, 1.0, 0.0).astype(BF16)
        for n in range(0, D, TN):
            x = zbuf[i, :, :, pl.ds(n, TN)].reshape(64, TN)
            picked = jnp.dot(chosen, x, preferred_element_type=F32) * scale
            picked = picked.astype(BF16)
            ybuf[i, 0, :, pl.ds(n, TN)] = picked[:16]
            ysend[i, :, :, pl.ds(n, TN)] = picked[16:].reshape(NY - 1, 16, TN)
        for r in range(1, NY):
            send(
                ysend.at[i, r - 1], ybuf.at[i, NY - r],
                y_ss.at[i, r - 1], y_rs.at[i, r - 1], y_to[r],
            )

    def part_rows(q):
        for i in (2 * q, 2 * q + 1):
            for r in range(1, NY):
                arrived(ybuf.at[i, NY - r], y_rs.at[i, r - 1], y_to[r])
        for r in range(NY):
            for n in range(0, D, TN):
                two = ybuf[pl.ds(2 * q, 2), r, :, pl.ds(n, TN)].astype(F32)
                at = pl.ds(r * 16, 16)
                rows_tok[q, at, pl.ds(n, TN)] = jnp.concatenate(
                    [two[0, :8], two[1, :8]], axis=0
                ).astype(BF16)
                rows_sc[q, at, pl.ds(n, TN)] = jnp.concatenate(
                    [two[0, 8:], two[1, 8:]], axis=0
                ).astype(BF16)
        send(rows_sc.at[q], rows_in.at[q], f_ss.at[q], f_rs.at[q], partner)

    def expert(q, nq):
        rows = nq * 64
        at_q = pl.ds(q, nq)
        for j in range(2):
            tok = rows_tok[at_q].reshape(rows, D)
            pre = jnp.dot(tok, gu[:, pl.ds(2 * H * j, 2 * H)], preferred_element_type=F32)
            pre_gate, pre_up = pre[:, :H], pre[:, H:]
            sig = jax.nn.sigmoid(pre_gate)
            activated = pre_gate * sig
            hidden = (activated * pre_up).astype(BF16)
            hidden_grad = nt(rows_sc[at_q].reshape(rows, D), down[pl.ds(H * j, H), :])
            gate_grad = hidden_grad * pre_up * sig * (1.0 + pre_gate * (1.0 - sig))
            both[j, pl.ds(0, rows), pl.ds(0, H)] = gate_grad.astype(BF16)
            both[j, pl.ds(0, rows), pl.ds(H, H)] = (hidden_grad * activated).astype(BF16)
            if j == 0:
                hid_own[at_q] = hidden.reshape(nq, 64, H)
            else:
                hid_send[at_q] = hidden.reshape(nq, 64, H)
            yield
        TW = min(TN, D2)
        for n in range(0, D, TW):
            at = pl.ds(n, TW)
            parts = [
                nt(both[j, pl.ds(0, rows)], gu[at, pl.ds(2 * H * j, 2 * H)])
                for j in range(2)
            ]
            parts = [p.astype(BF16).astype(F32) for p in parts]
            total = (parts[0] + parts[1]).astype(BF16).reshape(nq, 64, TW)
            ebuf[at_q, 0, :, at] = total[:, :16]
            esend[at_q, :, :, at] = total[:, 16:].reshape(nq, NY - 1, 16, TW)
            if (n + TW) % D2 == 0:
                for p in range(q, q + nq):
                    for r in (2, 1, 3):
                        send(*back(p, r, n // D2))
        for p in range(q, q + nq):
            send(hid_send.at[p], hid_in.at[p], p_ss.at[p], p_rs.at[p], partner)
        yield

    def back(q, r, c):
        at = pl.ds(c * D2, D2)
        src, dst = esend.at[q, r - 1, :, at], ebuf.at[q, NY - r, :, at]
        return src, dst, e_ss.at[q, r - 1, c], e_rs.at[q, r - 1, c], y_to[r]

    def down_grad():
        for q in range(Q):
            arrived(rows_in.at[q], f_rs.at[q], partner)
            arrived(hid_in.at[q], p_rs.at[q], partner)
        own = hid_own[...].reshape(Q * 64, H).astype(F32).T.astype(BF16)
        taken = hid_in[...].reshape(Q * 64, H).astype(F32).T.astype(BF16)
        for n in range(0, D, TN):
            at = pl.ds(n, TN)
            grad = jnp.dot(
                own, rows_sc[:, :, at].reshape(Q * 64, TN), preferred_element_type=F32
            )
            cur_ref[:, at] = grad + jnp.dot(
                taken, rows_in[:, :, at].reshape(Q * 64, TN), preferred_element_type=F32
            )

    def combine(q):
        for r in range(1, NY):
            for c in range(2):
                arrived(*back(q, r, c)[1::2], y_to[r])
        tokens = gbuf[pl.ds(2 * q, 2)].reshape(64, 128)
        table = nt(tokens, pick, precision=lax.Precision.HIGHEST)
        mine = (r64 // 8 == (c64 // 2) % 8) & (table > 0.0)
        chosen = jnp.where(mine, 1.0, 0.0).astype(BF16)
        for n in range(0, D, TN):
            x = ebuf[q, :, :, pl.ds(n, TN)].reshape(64, TN)
            total = jnp.dot(chosen, x, preferred_element_type=F32)
            cbuf[pl.ds(2 * q, 2), :, :, pl.ds(n, TN)] = total.reshape(2, 2, 16, TN)

    def chain(s, d, c):
        at = pl.ds(c * D2, D2)
        sem = (d, 0, s - 1, c)
        buf = (d, 0, s - 1, slice(None), at)
        return rsend.at[buf], rrecv.at[buf], r_ss.at[sem], r_rs.at[sem], z_two[d]

    def side(s, d):
        buf, sem = (d, 1, s - 1), (d, 1, s - 1, 0)
        return rsend.at[buf], rrecv.at[buf], r_ss.at[sem], r_rs.at[sem], z_to[d]

    def send_side(q):
        for d in range(2):
            rsend[d, 1, Q - q - 1] = cbuf[2 * q, 1 - d].astype(BF16)
            send(*side(Q - q, d))

    def got(copy):
        arrived(copy[1], copy[3], copy[4])

    def sum_z():
        for s in range(1, Q + 1):
            for d in range(2):
                if s > 1:
                    got(side(s - 1, d))
            for c in range(2):
                for d in range(2):
                    if s == 1 and c != d:
                        continue
                    at = pl.ds(c * D2, D2)
                    k = K + 2 - 2 * s
                    total = cbuf[k - 1, 1 if k == K else 1 - d, :, at]
                    if s > 1:
                        total = total + rrecv[d, 1, s - 2, :, at].astype(F32)
                    if s > 2 or (s == 2 and c == d):
                        got(chain(s - 1, d, c))
                        total = total + rrecv[d, 0, s - 2, :, at].astype(F32)
                    rsend[d, 0, s - 1, :, at] = total.astype(BF16)
                    send(*chain(s, d, c))
            yield
        for d in range(2):
            got(side(Q, d))
        for c in range(2):
            at = pl.ds(c * D2, D2)
            total = cbuf[K - 1, 0, :, at]
            for d in range(2):
                total = total + rrecv[d, 1, Q - 1, :, at].astype(F32)
                if Q > 1 or c == d:
                    got(chain(Q, d, c))
                    total = total + rrecv[d, 0, Q - 1, :, at].astype(F32)
            cot_ref[:, :, at] = total.reshape(2, 8, D2).astype(BF16)
        yield

    def newton():
        squares = jnp.zeros((8, 128), F32)
        for n in range(0, D, 128):
            piece = cur_ref[:, pl.ds(n, 128)]
            squares = squares + jnp.sum((piece * piece).reshape(H // 8, 8, 128), axis=0)
        nsend[...] = jnp.broadcast_to(jnp.sum(squares, keepdims=True), (8, 128))
        send(nsend, nrecv, n_ss, n_rs, partner)
        yield
        arrived(nrecv, n_rs, partner)
        norm = jnp.sqrt(nsend[...] + nrecv[...]) + 1e-07
        factor = (1.0 / norm)[:1, :1]
        for it in range(ITERS):
            mine = whole.at[it, me]
            for n in range(0, D, TN):
                at = pl.ds(n, TN)
                if it == 0:
                    value = cur_ref[:, at] * factor
                    cur_ref[:, at] = value
                    mine[:, at] = value.astype(BF16)
            send(mine, mine, x_ss.at[it], x_rs.at[it], partner)
            yield
            other = whole.at[it, 1 - me]
            gram_own = nt(mine[...], mine[...])
            yield
            arrived(other, x_rs.at[it], partner)
            gram_other = nt(mine[...], other[...])
            gm = gram_b.at[it, me]
            own_at = pl.ds(pl.multiple_of(me * H, H), H)
            other_at = pl.ds(pl.multiple_of((1 - me) * H, H), H)
            gm[:, own_at] = gram_own.astype(BF16)
            gm[:, other_at] = gram_other.astype(BF16)
            send(gm, gm, m_ss.at[it], m_rs.at[it], partner)
            yield
            arrived(gram_b.at[it, 1 - me], m_rs.at[it], partner)
            full = gram_b[it].reshape(2 * H, 2 * H)
            square = jnp.dot(gm[...], full, preferred_element_type=F32)
            sq_own = jnp.where(me == 0, square[:, :H], square[:, H:])
            sq_other = jnp.where(me == 0, square[:, H:], square[:, :H])
            p_own = (CUBIC * gram_own + QUINTIC * sq_own).astype(BF16)
            p_other = (CUBIC * gram_other + QUINTIC * sq_other).astype(BF16)
            yield
            for n in range(0, D, TN):
                at = pl.ds(n, TN)
                step = jnp.dot(p_own, mine[:, at], preferred_element_type=F32)
                step = step + jnp.dot(p_other, other[:, at], preferred_element_type=F32)
                value = LINEAR * cur_ref[:, at] + step
                if it + 1 < ITERS:
                    cur_ref[:, at] = value
                    whole.at[it + 1, me][:, at] = value.astype(BF16)
                else:
                    upd_ref[:, at] = (value * math.sqrt(max(2 * H, D))).astype(BF16)
            yield
        pltpu.make_async_copy(upd_ref, upd_hbm, o_sem.at[0]).start()

    shares = [
        (gate_hbm.at[0], gu.at[:, pl.ds(2 * H, H)]),
        (up_hbm.at[0], gu.at[:, pl.ds(3 * H, H)]),
        (down_hbm.at[0], down.at[pl.ds(H, H)]),
    ]
    for n, (src, dst) in enumerate(shares):
        send(src, dst, v_ss.at[n], v_rs.at[n], partner)

    def weights_here():
        for c in loads[4:]:
            c.wait()
        for n, (_, dst) in enumerate(shares):
            arrived(dst, v_rs.at[n], partner)

    early = max(0, Q - 2)
    first = iter(())
    for s in range(1, K + 1):
        for d, key in pieces:
            if goes(s, d, key):
                arrived(*hop(s, d, key)[1::2], z_to[d])
                if goes(s + 1, d, key):
                    send(*hop(s + 1, d, key))
        select(s - 1)
        if early and s == K - 2:
            weights_here()
            for q in range(early):
                part_rows(q)
            first = expert(0, early)
        advance(first, 1)
    advance(first, 3)
    if not early:
        weights_here()
    for q in range(early, Q):
        part_rows(q)
        advance(expert(q, 1), 3)
    for q in range(Q - 2):
        combine(q)
        send_side(q)
    down_grad()
    ns = newton()
    advance(ns, 1)
    combine(Q - 1)
    ring = sum_z()
    advance(ring, 1)
    send_side(Q - 1)
    if Q > 1:
        combine(Q - 2)
        send_side(Q - 2)
    for s in range(2, Q + 1):
        advance(ns, (2, 1, 4)[(s - 2) % 3])
        advance(ring, 1)
    advance(ns, 20)
    advance(ring, 2)
    cot_out = pltpu.make_async_copy(cot_ref, cot_hbm, o_sem.at[1])
    cot_out.start()
    for c in pending:
        c.wait_send()
    cot_out.wait()
    pltpu.make_async_copy(upd_ref, upd_hbm, o_sem.at[0]).wait()


def hand_over(cot_ref, upd_ref, cot_out, upd_out, cot_mem, upd_mem, in_sem, out_sem):
    rows = upd_mem.shape[0] // 4
    parts = [(cot_ref, cot_mem, cot_out)]
    for n in range(4):
        at = pl.ds(n * rows, rows)
        parts.append((upd_ref.at[at], upd_mem.at[at], upd_out.at[0, at]))
    into = [pltpu.make_async_copy(p[0], p[1], in_sem.at[n]) for n, p in enumerate(parts)]
    out = [pltpu.make_async_copy(p[1], p[2], out_sem.at[n]) for n, p in enumerate(parts)]
    for c in into:
        c.start()
    for c, o in zip(into, out):
        c.wait()
        o.start()
    for o in out:
        o.wait()


def on_device(activations, upstream, routes, route_gates, gate_matrix, up_matrix, down_matrix):
    NZ = lax.axis_size("expert") // NY
    K = NZ // 2
    Q = K // 2
    D = activations.shape[2]
    H = down_matrix.shape[1]
    dma = pltpu.SemaphoreType.DMA
    anywhere = pl.BlockSpec(memory_space=pl.ANY)
    args = (activations, upstream, routes, route_gates, gate_matrix, up_matrix, down_matrix)
    cot, upd = pl.pallas_call(
        functools.partial(kernel, NZ),
        out_shape=(
            jax.ShapeDtypeStruct((2, 8, D), BF16),
            jax.ShapeDtypeStruct((H, D), BF16),
        ),
        in_specs=[anywhere] * 7,
        out_specs=(anywhere, anywhere),
        scratch_shapes=[
            pltpu.VMEM(activations.shape, BF16),
            pltpu.VMEM(upstream.shape, BF16),
            pltpu.VMEM(routes.shape, routes.dtype),
            pltpu.VMEM(route_gates.shape, F32),
            pltpu.VMEM((2, 8, D), BF16),
            pltpu.VMEM((H, D), BF16),
            pltpu.VMEM((H, D), F32),
            pltpu.VMEM((Q, 64, H), BF16),
            pltpu.VMEM((Q, 64, H), BF16),
            pltpu.VMEM((Q, 64, H), BF16),
            pltpu.VMEM((2, max(1, Q - 2) * 64, 2 * H), BF16),
            pltpu.VMEM((K, 2, 32, D), BF16),
            pltpu.VMEM((K, 2, 16, 128), F32),
            pltpu.VMEM((K, NY - 1, 16, D), BF16),
            pltpu.VMEM((K, NY, 16, D), BF16),
            pltpu.VMEM((Q, 64, D), BF16),
            pltpu.VMEM((Q, 64, D), BF16),
            pltpu.VMEM((Q, 64, D), BF16),
            pltpu.VMEM((D, 4 * H), BF16),
            pltpu.VMEM((2 * H, D), BF16),
            pltpu.VMEM((Q, NY - 1, 16, D), BF16),
            pltpu.VMEM((Q, NY, 16, D), BF16),
            pltpu.VMEM((K, 2, 16, D), F32),
            pltpu.VMEM((2, 2, Q, 16, D), BF16),
            pltpu.VMEM((2, 2, Q, 16, D), BF16),
            pltpu.VMEM((8, 128), F32),
            pltpu.VMEM((8, 128), F32),
            pltpu.VMEM((ITERS, 2, H, D), BF16),
            pltpu.VMEM((ITERS, 2, H, 2 * H), BF16),
            dma((7,)), dma((2,)),
            dma((2, K, 4)), dma((2, K, 4)),
            dma((2, K)), dma((2, K)),
            dma((K, NY - 1)), dma((K, NY - 1)),
            dma((Q,)), dma((Q,)),
            dma((Q,)), dma((Q,)),
            dma((3,)), dma((3,)),
            dma((Q, NY - 1, 2)), dma((Q, NY - 1, 2)),
            dma((2, 2, Q, 2)), dma((2, 2, Q, 2)),
            dma(()), dma(()),
            dma((ITERS,)), dma((ITERS,)),
            dma((ITERS,)), dma((ITERS,)),
        ],
        compiler_params=pltpu.CompilerParams(collective_id=0, has_side_effects=True),
    )(*args)
    return pl.pallas_call(
        hand_over,
        out_shape=(
            jax.ShapeDtypeStruct((2, 8, D), BF16),
            jax.ShapeDtypeStruct((1, H, D), BF16),
        ),
        in_specs=[anywhere] * 2,
        out_specs=(anywhere, anywhere),
        scratch_shapes=[
            pltpu.VMEM((2, 8, D), BF16), pltpu.VMEM((H, D), BF16), dma((5,)), dma((5,)),
        ],
    )(cot, upd)


def solution(mesh):
    rows = P(None, ("dp", "expert", "half"), None)
    return jax.shard_map(
        on_device,
        mesh=mesh,
        in_specs=(
            rows, rows, rows, rows,
            P("expert", None, "half"), P("expert", None, "half"), P("expert", "half", None),
        ),
        out_specs=(rows, P(("dp", "expert"), "half", None)),
        check_vma=False,
    )
```
